32 devices in a mesh: sec: 2 (over x), blk: 8 (over z, y), mp: 2 (over core).
Axes of the slice: x: 2, y: 2, z: 4, core: 2. Of those that a mesh axis runs over, the one named last changes fastest.
Arguments:
- image_pooled: bfloat16 [1536, 1536], P('blk', ('sec', 'mp')), may hold values from -4 to 4
- text_pooled: bfloat16 [1536, 2048], P('blk', ('sec', 'mp')), may hold values from -4 to 4
- image_proj: bfloat16 [1536, 1152], P(('sec', 'mp')), may hold values from -0.15625 to 0.15625
- text_proj: bfloat16 [2048, 1152], P(('sec', 'mp')), may hold values from -0.125 to 0.125
- natural_log_multiplier: float32 [1], replicated, may hold values from 1.4 to 2.3
- logit_bias: float32 [1], replicated, may hold values from -2 to -0.5
- match_cluster_labels: int32 [1536], P('blk'), may hold values from 0 to 1535
Outputs:
- pair_loss: float32 [2, 1536], P('sec', 'blk')
- image_grad: bfloat16 [1536, 1536], P('blk', ('sec', 'mp'))
- text_grad: bfloat16 [1536, 2048], P('blk', ('sec', 'mp'))
The draws below stay inside these ranges and needn't reach their ends.
All inputs are finite; a program needn't handle non-finite values.
Results may differ from the reference program's by a relative error of at most 0.0065.
Values may be sent and summed in bfloat16 or wider, within the bound.
No kernel may reach another device: no remote copies, remote signals or barrier semaphores. Data moves between devices by JAX's collectives and lax.ppermute only.
A program may use at most 128 MiB of HBM per device.

```python
import math
import jax
import jax.numpy as jnp
from jax import lax

DI = 1536
DT = 2048
EMB = 1152
PAIRS = 1536


def draw_features(key, row_count, feature_count):
    subkeys = jax.random.split(key, 3)
    normal_part = jax.random.truncated_normal(subkeys[0], -6.0, 6.0, (row_count, feature_count), jnp.float32)
    row_scale = jnp.exp(jax.random.uniform(subkeys[1], (row_count, 1), jnp.float32, math.log(0.005), math.log(0.05)))
    col_scale = jnp.exp(jax.random.uniform(subkeys[2], (1, feature_count), jnp.float32, 0.0, math.log(10.0)))
    return jnp.clip(normal_part * row_scale * col_scale, -4.0, 4.0).astype(jnp.bfloat16)


def draw_image_pooled(key, part):
    return draw_features(jax.random.fold_in(key, 11), PAIRS, DI)


def draw_text_pooled(key, part):
    return draw_features(jax.random.fold_in(key, 12), PAIRS, DT)


def place_ends(values, stream_key, low, top_value):
    shape = values.shape
    index_at = [jax.random.randint(jax.random.fold_in(stream_key, axis), (), 0, shape[axis]) for axis in range(len(shape))]
    values = values.at[tuple(index_at)].set(low)
    longest = shape.index(max(shape))
    index_at[longest] = (index_at[longest] + 1) % shape[longest]
    return values.at[tuple(index_at)].set(top_value)


def shard_levels(own_key, extent, cuts, smallest, top_value):
    gain, own = 1.0, jax.random.fold_in(own_key, 6)
    for position, shards_of in cuts:
        draws = jnp.exp(jax.random.uniform(jax.random.fold_in(own, position), (shards_of,), jnp.float32, smallest / len(cuts), top_value / len(cuts)))
        gain = gain * jnp.repeat(draws, extent[position] // shards_of).reshape([-1 if axis == position else 1 for axis in range(len(extent))])
    return gain


def normal_values(key, extent, width, reach, cuts=(), held_as=jnp.bfloat16):
    drawn = jax.random.normal(key, extent, jnp.float32) * width
    if len(cuts) > 0:
        drawn = shard_levels(key, extent, cuts, -0.22, 0.18) * drawn
    return jnp.clip(drawn, min=-reach, max=reach).astype(held_as)


def setup_inputs(seed: int = 0) -> dict:
    keys = jax.random.split(jax.random.key(seed), 8)
    image_pooled = draw_image_pooled(jax.random.fold_in(keys[7], 71), 0)
    text_pooled = draw_text_pooled(jax.random.fold_in(keys[7], 71), 0)
    image_proj = normal_values(keys[2], (DI, EMB), DI ** -0.5, 0.15625, ((0, 4),))
    text_proj = normal_values(keys[3], (DT, EMB), DT ** -0.5, 0.125, ((0, 4),))
    natural_log_multiplier = jnp.clip(jax.random.uniform(keys[4], (1,), jnp.float32, 1.4, 2.3), 1.4, 2.3)
    logit_bias = jnp.clip(jax.random.uniform(keys[5], (1,), jnp.float32, -2.0, -0.5), -2.0, -0.5)
    match_cluster_labels = place_ends(jax.random.randint(keys[6], (PAIRS,), 0, PAIRS), jax.random.fold_in(keys[6], 1), 0, PAIRS - 1).astype(jnp.int32)
    return {"image_pooled": image_pooled, "text_pooled": text_pooled, "image_proj": image_proj, "text_proj": text_proj, "natural_log_multiplier": natural_log_multiplier, "logit_bias": logit_bias, "match_cluster_labels": match_cluster_labels}


def unit_rows(embedding):
    row_norm = jnp.sqrt(lax.optimization_barrier(jnp.sum(embedding * embedding, axis=1, keepdims=True)) + 1e-06)
    return (embedding / row_norm, row_norm)

def sideways_contributions(resident_slice, counterpart_slice, match_cluster_labels, sharpness_factor, shift_quantity):
    row_count = resident_slice.shape[0]
    block_rows = math.gcd(row_count, 512)
    own_blocks = resident_slice.reshape(row_count // block_rows, block_rows, resident_slice.shape[1])
    id_blocks = match_cluster_labels.reshape(row_count // block_rows, block_rows)

    def block_terms(inputs_pair):
        rescaled_slice, id_block = inputs_pair
        agreement_scores_matrix = sharpness_factor * lax.dot_general(rescaled_slice, counterpart_slice, (((1,), (1,)), ((), ())), preferred_element_type=jnp.float32) + shift_quantity
        desired_polarity = jnp.where(id_block[:, None] == match_cluster_labels[None, :], 1.0, -1.0).astype(jnp.float32)
        row_losses = lax.optimization_barrier(jnp.sum(jax.nn.softplus(-desired_polarity * agreement_scores_matrix), axis=1))
        penalty_factor = (-sharpness_factor * desired_polarity * jax.nn.sigmoid(-desired_polarity * agreement_scores_matrix)).astype(jnp.bfloat16)
        unit_grad = jnp.dot(penalty_factor, counterpart_slice, preferred_element_type=jnp.float32)
        return (row_losses, unit_grad)
    row_losses, unit_grad = lax.map(block_terms, (own_blocks, id_blocks))
    return (row_losses.reshape(row_count), unit_grad.reshape(row_count, resident_slice.shape[1]))

def backward_unit(unit, row_norm, unit_grad):
    projection = lax.optimization_barrier(jnp.sum(unit * unit_grad, axis=1, keepdims=True))
    return ((unit_grad - unit * projection) / row_norm).astype(jnp.bfloat16)

def reference(image_pooled, text_pooled, image_proj, text_proj, natural_log_multiplier, logit_bias, match_cluster_labels):
    image_emb = jnp.dot(image_pooled, image_proj, preferred_element_type=jnp.float32)
    text_emb = jnp.dot(text_pooled, text_proj, preferred_element_type=jnp.float32)
    image_unit, image_norm = unit_rows(image_emb)
    text_unit, text_norm = unit_rows(text_emb)
    photo_rows_slice = image_unit.astype(jnp.bfloat16)
    sentence_rows_slice = text_unit.astype(jnp.bfloat16)
    sharpness_factor = jnp.exp(natural_log_multiplier[0])
    shift_quantity = logit_bias[0]
    photo_cost, photo_direction_derivative = sideways_contributions(photo_rows_slice, sentence_rows_slice, match_cluster_labels, sharpness_factor, shift_quantity)
    sentence_cost, sentence_direction_derivative = sideways_contributions(sentence_rows_slice, photo_rows_slice, match_cluster_labels, sharpness_factor, shift_quantity)
    image_demb = backward_unit(image_unit, image_norm, photo_direction_derivative)
    text_demb = backward_unit(text_unit, text_norm, sentence_direction_derivative)
    image_grad = lax.dot_general(image_demb, image_proj, (((1,), (1,)), ((), ())), preferred_element_type=jnp.float32).astype(jnp.bfloat16)
    text_grad = lax.dot_general(text_demb, text_proj, (((1,), (1,)), ((), ())), preferred_element_type=jnp.float32).astype(jnp.bfloat16)
    pair_loss = jnp.stack([photo_cost, sentence_cost])
    return (pair_loss, image_grad, text_grad)
```

```python
import jax
import jax.numpy as jnp
from jax import lax
from jax.experimental import pallas as pl
from jax.experimental.pallas import tpu as pltpu
from jax.sharding import PartitionSpec as P

F32 = jnp.float32
BF16 = jnp.bfloat16
SWAP = [(0, 1), (1, 0)]
NT = (((1,), (1,)), ((), ()))
VMEM_LIMIT = 40 * 1024 * 1024


def local_call(kernel, name, outs, scalars, arrays, scratch=(), flops=0, transcendentals=0):
    nbytes = sum(a.size * a.dtype.itemsize for a in arrays)
    return pl.pallas_call(
        kernel,
        out_shape=outs,
        in_specs=[pl.BlockSpec(memory_space=pltpu.SMEM)] * len(scalars)
        + [pl.BlockSpec(memory_space=pltpu.VMEM)] * len(arrays),
        out_specs=[pl.BlockSpec(memory_space=pltpu.VMEM)] * len(outs),
        scratch_shapes=list(scratch),
        compiler_params=pltpu.CompilerParams(vmem_limit_bytes=VMEM_LIMIT),
        cost_estimate=pl.CostEstimate(
            flops=flops, bytes_accessed=nbytes, transcendentals=transcendentals
        ),
        name=name,
    )(*scalars, *arrays)


def half_embed_kernel(which, dtype):
    def kernel(place, image_pooled, text_pooled, image_proj, text_proj, out):
        half = out.shape[1]
        core = place[2]
        start = pl.multiple_of((core if which == 0 else 1 - core) * half, half)
        rows = pl.ds(start, half)
        out[0] = jnp.dot(
            image_pooled[rows, :], image_proj[...], preferred_element_type=F32
        ).astype(dtype)
        out[1] = jnp.dot(
            text_pooled[rows, :], text_proj[...], preferred_element_type=F32
        ).astype(dtype)

    return kernel


def join_cores_kernel(place, kept, got, own_sum, other_sum, own_send, other_send):
    section = place[0]
    own = kept[section] + got[section].astype(F32)
    own_sum[...] = own
    own_send[...] = own.astype(BF16)
    other = kept[1 - section] + got[1 - section].astype(F32)
    other_sum[...] = other
    other_send[...] = other.astype(BF16)


def unit_kernel(summed, got, unit, unit_b, norm):
    emb = summed[...] + got[...].astype(F32)
    row_norm = jnp.sqrt(jnp.sum(emb * emb, axis=1, keepdims=True) + 1e-06)
    value = emb / row_norm
    unit[...] = value
    unit_b[...] = value.astype(BF16)
    norm[...] = row_norm


def pair_kernel(blocks, first, last):
    def kernel(place, scale_bias, own_a, own_b, own_ids, visit_ids, *refs):
        pieces = refs[: 2 * blocks]
        refs = refs[2 * blocks :]
        if not first:
            grad_in, loss_in = refs[:2]
            refs = refs[2:]
        if last:
            grad_keep, grad_own, grad_near, loss_own, loss_near = refs[:5]
            refs = refs[5:]
        else:
            grad_out, loss_out = refs[:2]
            refs = refs[2:]
        own, visited = refs
        half = own_a.shape[0]
        core = place[2]
        own[pl.ds(0, half), :] = own_a[...]
        own[pl.ds(half, half), :] = own_b[...]
        for block in range(blocks):
            mine = pl.multiple_of(core * half, half) + 2 * half * block
            theirs = pl.multiple_of((1 - core) * half, half) + 2 * half * block
            visited[pl.ds(mine, half), :] = pieces[2 * block][...]
            visited[pl.ds(theirs, half), :] = pieces[2 * block + 1][...]
        scale = scale_bias[0]
        scores = (
            scale * lax.dot_general(own[...], visited[...], NT, preferred_element_type=F32)
            + scale_bias[1]
        )
        sign = jnp.where(own_ids[...] == visit_ids[...], 1.0, -1.0).astype(F32)
        value = -sign * scores
        small = jnp.exp(-jnp.abs(value))
        losses = jnp.maximum(value, 0.0) + jnp.log1p(small)
        sigmoid = jnp.where(value >= 0.0, 1.0, small) / (1.0 + small)
        weight = (-scale * sign * sigmoid).astype(BF16)
        grad = jnp.dot(weight, visited[...], preferred_element_type=F32)
        loss = jnp.sum(losses, axis=1, keepdims=True)
        if not first:
            grad = grad + grad_in[...]
            loss = loss + loss_in[...]
        if last:
            grad_keep[...] = grad[:half]
            grad_own[...] = grad[:half].astype(BF16)
            grad_near[...] = grad[half:].astype(BF16)
            wide = jnp.broadcast_to(loss, (2 * half, 128))
            loss_own[...] = jnp.transpose(wide[:half])[0:1]
            loss_near[...] = jnp.transpose(wide[half:])[0:1]
        else:
            grad_out[...] = grad
            loss_out[...] = loss

    return kernel


def demb_kernel(place, kept, near, across, diagonal, own_unit, own_norm, other_unit, other_norm, out):
    section = place[0]

    def finish(grad, unit, norm):
        value = unit[...]
        along = jnp.sum(value * grad, axis=1, keepdims=True)
        return ((grad - value * along) / norm[...]).astype(BF16)

    out[section] = finish(kept[...] + near[...].astype(F32), own_unit, own_norm)
    out[1 - section] = finish(
        across[...].astype(F32) + diagonal[...].astype(F32), other_unit, other_norm
    )


def grads_kernel(place, mine, theirs, image_proj, text_proj, image_grad, text_grad):
    half = mine.shape[1]
    core = place[2]
    for place_of, source in ((core, mine), (1 - core, theirs)):
        rows = pl.ds(pl.multiple_of(place_of * half, half), half)
        image_grad[rows, :] = lax.dot_general(
            source[0], image_proj[...], NT, preferred_element_type=F32
        ).astype(BF16)
        text_grad[rows, :] = lax.dot_general(
            source[1], text_proj[...], NT, preferred_element_type=F32
        ).astype(BF16)


def make_per_device(mesh):
    sections = mesh.shape["sec"]
    blocks = mesh.shape["blk"]

    def across_blk(value, step):
        return lax.ppermute(value, "blk", [(i, i ^ step) for i in range(blocks)])

    def per_device(
        image_pooled, text_pooled, image_proj, text_proj, log_multiplier, logit_bias, ids
    ):
        section = lax.axis_index("sec")
        core = lax.axis_index("mp")
        place = jnp.stack([section, lax.axis_index("blk"), core]).astype(jnp.int32)
        scale_bias = jnp.concatenate([jnp.exp(log_multiplier), logit_bias])
        rows = image_pooled.shape[0]
        half = rows // 2
        width = image_proj.shape[1]
        block_f32 = jax.ShapeDtypeStruct((half, width), F32)
        block_b16 = jax.ShapeDtypeStruct((half, width), BF16)
        norm_shape = jax.ShapeDtypeStruct((half, 1), F32)
        towers = (image_pooled, text_pooled, image_proj, text_proj)
        embed_flops = 2 * half * width * (image_proj.shape[0] + text_proj.shape[0])

        (sent,) = local_call(
            half_embed_kernel(1, BF16),
            "embed_sent",
            [jax.ShapeDtypeStruct((2, half, width), BF16)],
            [place],
            towers,
            flops=embed_flops,
        )
        got = lax.ppermute(sent, "mp", SWAP)
        (kept,) = local_call(
            half_embed_kernel(0, F32),
            "embed_kept",
            [jax.ShapeDtypeStruct((2, half, width), F32)],
            [place],
            towers,
            flops=embed_flops,
        )
        own_sum, other_sum, own_send, other_send = local_call(
            join_cores_kernel,
            "join_cores",
            [block_f32, block_f32, block_b16, block_b16],
            [place],
            [kept, got],
        )
        other_got = lax.ppermute(own_send, "sec", SWAP)
        own_got = lax.ppermute(other_send, "sec", SWAP)
        other_unit, visit, other_norm = local_call(
            unit_kernel, "other_unit", [block_f32, block_b16, norm_shape], [], [other_sum, other_got]
        )
        own_unit, own_rows, own_norm = local_call(
            unit_kernel, "own_unit", [block_f32, block_b16, norm_shape], [], [own_sum, own_got]
        )

        steps = list(range(0, blocks, 2))
        mine = [visit] + [across_blk(visit, k) for k in steps[1:]]
        near_rows = across_blk(own_rows, 1)
        ids_row = ids[None, :]
        ids_row, _ = lax.optimization_barrier((ids_row, own_rows))
        near_ids = across_blk(ids_row, 1)
        block_ids = [ids_row] + [across_blk(ids_row, k) for k in steps[1:]]
        theirs = [lax.ppermute(v, "mp", SWAP) for v in mine]

        own_ids = jnp.concatenate(
            [
                lax.dynamic_slice_in_dim(ids_row, core * half, half, 1),
                lax.dynamic_slice_in_dim(near_ids, core * half, half, 1),
            ],
            axis=1,
        ).reshape(2 * half, 1)
        groups = [list(range(i, min(i + 2, len(steps)))) for i in range(0, len(steps), 2)]
        state = []
        for index, group in enumerate(groups):
            first, last = index == 0, index == len(groups) - 1
            visit_ids = jnp.concatenate([block_ids[g] for g in group], axis=1)
            pieces = [p for g in group for p in (mine[g], theirs[g])]
            if last:
                outs = [block_f32, block_b16, block_b16]
                outs += [jax.ShapeDtypeStruct((1, half), F32)] * 2
            else:
                outs = [
                    jax.ShapeDtypeStruct((2 * half, width), F32),
                    jax.ShapeDtypeStruct((2 * half, 1), F32),
                ]
            visited_rows = 2 * half * len(group)
            state = local_call(
                pair_kernel(len(group), first, last),
                "pairs",
                outs,
                [place, scale_bias],
                [own_rows, near_rows, own_ids, visit_ids, *pieces, *state],
                scratch=[
                    pltpu.VMEM((2 * half, width), BF16),
                    pltpu.VMEM((visited_rows, width), BF16),
                ],
                flops=8 * half * visited_rows * width,
                transcendentals=6 * half * visited_rows,
            )
        grad_keep, grad_own, grad_near, loss_own, loss_near = state

        pairs = [(s, b) for s in range(sections) for b in range(blocks)]
        diagonal_pairs = [
            (s * blocks + b, (1 - s) * blocks + (b ^ 1)) for s, b in pairs
        ]
        near = across_blk(grad_near, 1)
        diagonal = lax.ppermute(grad_near, ("sec", "blk"), diagonal_pairs)
        across = lax.ppermute(grad_own, "sec", SWAP)
        (demb,) = local_call(
            demb_kernel,
            "demb",
            [jax.ShapeDtypeStruct((2, half, width), BF16)],
            [place],
            [grad_keep, near, across, diagonal, own_unit, own_norm, other_unit, other_norm],
        )
        demb_got = lax.ppermute(demb, "mp", SWAP)
        loss_mine = loss_own + across_blk(loss_near, 1)
        loss_theirs = lax.ppermute(loss_mine, "mp", SWAP)
        pair_loss = jnp.where(
            core == 0,
            jnp.concatenate([loss_mine, loss_theirs], axis=1),
            jnp.concatenate([loss_theirs, loss_mine], axis=1),
        )
        image_grad, text_grad = local_call(
            grads_kernel,
            "grads",
            [
                jax.ShapeDtypeStruct((rows, image_proj.shape[0]), BF16),
                jax.ShapeDtypeStruct((rows, text_proj.shape[0]), BF16),
            ],
            [place],
            [demb, demb_got, image_proj, text_proj],
            flops=2 * embed_flops,
        )
        return (pair_loss, image_grad, text_grad)

    return per_device


def solution(mesh):
    placed = (
        P("blk", ("sec", "mp")),
        P("blk", ("sec", "mp")),
        P(("sec", "mp"), None),
        P(("sec", "mp"), None),
        P(),
        P(),
        P("blk"),
    )
    return jax.shard_map(
        make_per_device(mesh),
        mesh=mesh,
        in_specs=placed,
        out_specs=(P("sec", "blk"), P("blk", ("sec", "mp")), P("blk", ("sec", "mp"))),
        check_vma=False,
    )
```

```python
import jax
import jax.numpy as jnp
from jax import lax
from jax.experimental import pallas as pl
from jax.experimental.pallas import tpu as pltpu
from jax.sharding import PartitionSpec as P

F32 = jnp.float32
BF16 = jnp.bfloat16
SWAP = [(0, 1), (1, 0)]
NT = (((1,), (1,)), ((), ()))
VMEM_LIMIT = 16 * 1024 * 1024
LANES = 128
EXTRA = 8


def local_call(
    kernel, name, outs, scalars, arrays, scratch=(), flops=0, transcendentals=0, held=(),
):
    nbytes = sum(a.size * a.dtype.itemsize for a in (*arrays, *held))
    return pl.pallas_call(
        kernel,
        out_shape=outs,
        in_specs=[pl.BlockSpec(memory_space=pltpu.SMEM)] * len(scalars)
        + [pl.BlockSpec(memory_space=pltpu.VMEM)] * len(arrays)
        + [pl.BlockSpec(memory_space=pltpu.HBM)] * len(held),
        out_specs=[pl.BlockSpec(memory_space=pltpu.VMEM)] * len(outs),
        scratch_shapes=list(scratch),
        compiler_params=pltpu.CompilerParams(vmem_limit_bytes=VMEM_LIMIT),
        cost_estimate=pl.CostEstimate(
            flops=flops, bytes_accessed=nbytes, transcendentals=transcendentals
        ),
        name=name,
    )(*scalars, *arrays, *held)


def cuts(rows):
    size = 128 if rows % 128 == 0 else rows
    return [(start, size) for start in range(0, rows, size)]


def embed_rows(which, place, image_pooled, text_pooled, image_proj, text_proj, out, before):
    half = out.shape[1]
    core = place[2]
    start = pl.multiple_of((core if which == 0 else 1 - core) * half, half)
    rows = pl.ds(start, half)
    for index, (pooled, proj) in enumerate(
        ((image_pooled, image_proj), (text_pooled, text_proj))
    ):
        for copy in before[index]:
            copy.wait()
        out[index] = jnp.dot(pooled[rows, :], proj[...], preferred_element_type=F32).astype(
            out.dtype
        )


def embed_sent_kernel(place, *refs):
    sources, sent, held, sems = refs[:4], refs[4], refs[5:9], refs[9]
    before = [[], []]
    count = 0
    for index in (0, 2, 1, 3):
        source, target = sources[index], held[index]
        for start, size in cuts(source.shape[0]):
            rows = pl.ds(start, size)
            copy = pltpu.make_async_copy(source.at[rows], target.at[rows], sems.at[count])
            copy.start()
            before[index % 2].append(copy)
            count += 1
    embed_rows(1, place, *held, sent, before)


def embed_kept_kernel(place, *refs):
    embed_rows(0, place, *refs[:4], refs[4], [[], []])


def join_cores_kernel(place, kept, got, own_send, other_send):
    section = place[0]
    own_send[...] = (kept[section] + got[section].astype(F32)).astype(BF16)
    other_send[...] = (kept[1 - section] + got[1 - section].astype(F32)).astype(BF16)


def write_block(block, value, extra):
    half, width = value.shape
    for c in range(width // LANES):
        block[pl.ds(c * half, half), :] = value[:, c * LANES : (c + 1) * LANES].astype(BF16)
    block[pl.ds(half * (width // LANES), EXTRA), :] = extra.astype(BF16)


def read_block(block, target, start, half):
    for c in range(target.shape[1] // LANES):
        target[pl.ds(start, half), pl.ds(c * LANES, LANES)] = block[pl.ds(c * half, half), :]


def extra_rows(block):
    return block[pl.ds(block.shape[0] - EXTRA, EXTRA), :].astype(F32)


def block_ids(block):
    extra = extra_rows(block)
    return extra[0:1] * 128.0 + extra[1:2]


def split_rows(row, extra):
    high = row.astype(BF16).astype(F32)
    rest = row - high
    middle = rest.astype(BF16).astype(F32)
    extra[...] = jnp.zeros_like(extra)
    for index, part in enumerate((high, middle, rest - middle)):
        extra[index : index + 1, 0 : row.shape[1]] = part


def unit_kernel(own):
    def kernel(place, kept, got, summed, extra, unit, block, norm):
        section = place[0] if own else 1 - place[0]
        emb = kept[section] + got[section].astype(F32) + summed[...].astype(F32)
        row_norm = jnp.sqrt(jnp.sum(emb * emb, axis=1, keepdims=True) + 1e-06)
        value = emb / row_norm
        unit[...] = value
        norm[...] = row_norm
        write_block(block, value, extra[...].astype(F32))

    return kernel


def pair_kernel(blocks, first, last):
    def kernel(scale_bias, own_block, near_block, own_ids, *refs):
        pieces = refs[: 2 * blocks]
        refs = refs[2 * blocks :]
        if not first:
            grad_in, loss_in = refs[:2]
            refs = refs[2:]
        if last:
            grad_keep, grad_own, grad_near, loss_own = refs[:4]
            refs = refs[4:]
        else:
            grad_out, loss_out = refs[:2]
            refs = refs[2:]
        own, visited, visit_ids, extra = refs
        half = own.shape[0] // 2
        read_block(own_block, own, 0, half)
        read_block(near_block, own, half, half)
        for index, piece in enumerate(pieces):
            read_block(piece, visited, index * half, half)
            visit_ids[0:1, pl.ds(index * half, half)] = block_ids(piece)[:, :half]
        near_ids = jnp.transpose(jnp.broadcast_to(block_ids(near_block), (LANES, LANES)))
        ids = jnp.concatenate([own_ids[...], near_ids[:half, 0:1]], axis=0)
        scale = scale_bias[0]
        scores = (
            scale * lax.dot_general(own[...], visited[...], NT, preferred_element_type=F32)
            + scale_bias[1]
        )
        sign = jnp.where(ids == visit_ids[0:1, :], 1.0, -1.0).astype(F32)
        value = -sign * scores
        small = jnp.exp(-jnp.abs(value))
        losses = jnp.maximum(value, 0.0) + jnp.log1p(small)
        sigmoid = jnp.where(value >= 0.0, 1.0, small) / (1.0 + small)
        weight = (-scale * sign * sigmoid).astype(BF16)
        grad = jnp.dot(weight, visited[...], preferred_element_type=F32)
        loss = jnp.sum(losses, axis=1, keepdims=True)
        if not first:
            grad = grad + grad_in[...]
            loss = loss + loss_in[...]
        if last:
            grad_keep[...] = grad[:half]
            grad_own[...] = grad[:half].astype(BF16)
            wide = jnp.broadcast_to(loss, (2 * half, LANES))
            loss_own[...] = jnp.transpose(wide[:half])[0:1]
            split_rows(jnp.transpose(wide[half:])[0:1], extra)
            write_block(grad_near, grad[half:], extra[...])
        else:
            grad_out[...] = grad
            loss_out[...] = loss

    return kernel


def demb_kernel(
    place, kept, near, across, diagonal, own_unit, own_norm, other_unit, other_norm, loss_own,
    out, loss_mine, joined, extra,
):
    section = place[0]
    half, width = own_unit.shape

    def finish(grad, unit, norm):
        value = unit[...]
        along = jnp.sum(value * grad, axis=1, keepdims=True)
        return ((grad - value * along) / norm[...]).astype(BF16)

    rows = pl.ds(0, half)
    read_block(diagonal, joined, 0, half)
    out[1 - section, rows, :] = finish(
        across[...].astype(F32) + joined[...].astype(F32), other_unit, other_norm
    )
    read_block(near, joined, 0, half)
    out[section, rows, :] = finish(kept[...] + joined[...].astype(F32), own_unit, own_norm)
    parts = extra_rows(near)
    loss = loss_own[...] + (parts[0:1] + parts[1:2] + parts[2:3])[:, :half]
    loss_mine[...] = loss
    split_rows(loss, extra)
    out[:, pl.ds(half, EXTRA), :] = jnp.zeros((2, EXTRA, width), BF16)
    out[0, pl.ds(half, EXTRA), pl.ds(0, LANES)] = extra[...].astype(BF16)


def grads_kernel(
    place, mine, theirs, loss_mine, image_proj, text_proj, pair_loss, image_grad, text_grad, joined
):
    half = joined.shape[0] // 2
    core = place[2]
    for index, (proj, grad) in enumerate(((image_proj, image_grad), (text_proj, text_grad))):
        for spot, source in ((core, mine), (1 - core, theirs)):
            rows = pl.ds(pl.multiple_of(spot * half, half), half)
            joined[rows, :] = source[index, pl.ds(0, half), :]
        grad[...] = lax.dot_general(
            joined[...], proj[...], NT, preferred_element_type=F32
        ).astype(BF16)
    parts = theirs[0, pl.ds(half, EXTRA), pl.ds(0, LANES)].astype(F32)
    loss = loss_mine[...]
    loss_theirs = (parts[0:1] + parts[1:2] + parts[2:3])[:, :half]
    pair_loss[0:1, 0:half] = jnp.where(core == 0, loss, loss_theirs)
    pair_loss[0:1, half : 2 * half] = jnp.where(core == 0, loss_theirs, loss)


def make_per_device(mesh):
    sections = mesh.shape["sec"]
    blocks = mesh.shape["blk"]

    def across_blk(value, step):
        return lax.ppermute(value, "blk", [(i, i ^ step) for i in range(blocks)])

    def per_device(
        image_pooled, text_pooled, image_proj, text_proj, log_multiplier, logit_bias, ids
    ):
        section = lax.axis_index("sec")
        core = lax.axis_index("mp")
        place = jnp.stack([section, lax.axis_index("blk"), core]).astype(jnp.int32)
        scale_bias = jnp.concatenate([jnp.exp(log_multiplier), logit_bias])
        rows = image_pooled.shape[0]
        half = rows // 2
        width = image_proj.shape[1]
        block_rows = half * (width // LANES) + EXTRA
        whole_f32 = jax.ShapeDtypeStruct((half, width), F32)
        whole_b16 = jax.ShapeDtypeStruct((half, width), BF16)
        block_b16 = jax.ShapeDtypeStruct((block_rows, LANES), BF16)
        norm_shape = jax.ShapeDtypeStruct((half, 1), F32)
        loss_shape = jax.ShapeDtypeStruct((1, half), F32)
        towers = (image_pooled, text_pooled, image_proj, text_proj)
        embed_flops = 2 * half * width * (image_proj.shape[0] + text_proj.shape[0])

        half_ids = lax.dynamic_slice_in_dim(ids, core * half, half)
        digits = jnp.stack([half_ids >> 7, half_ids & 127]).astype(BF16)
        extra = jnp.pad(digits, ((0, EXTRA - 2), (0, LANES - half)))
        own_ids = half_ids.astype(F32).reshape(half, 1)

        copies = sum(len(cuts(t.shape[0])) for t in towers)
        sent, *towers = local_call(
            embed_sent_kernel,
            "embed_sent",
            [jax.ShapeDtypeStruct((2, half, width), BF16)]
            + [jax.ShapeDtypeStruct(t.shape, t.dtype) for t in towers],
            [place],
            [],
            scratch=[pltpu.SemaphoreType.DMA((copies,))],
            flops=embed_flops,
            held=[pltpu.with_memory_space_constraint(t, pltpu.HBM) for t in towers],
        )
        image_proj, text_proj = towers[2:]
        got = lax.ppermute(sent, "mp", SWAP)
        (kept,) = local_call(
            embed_kept_kernel,
            "embed_kept",
            [jax.ShapeDtypeStruct((2, half, width), F32)],
            [place],
            towers,
            flops=embed_flops,
        )
        own_send, other_send = local_call(
            join_cores_kernel, "join_cores", [whole_b16, whole_b16], [place], [kept, got]
        )
        other_got = lax.ppermute(own_send, "sec", SWAP)
        own_got = lax.ppermute(other_send, "sec", SWAP)
        other_unit, visit, other_norm = local_call(
            unit_kernel(False),
            "other_unit",
            [whole_f32, block_b16, norm_shape],
            [place],
            [kept, got, other_got, extra],
        )
        own_unit, own_block, own_norm = local_call(
            unit_kernel(True),
            "own_unit",
            [whole_f32, block_b16, norm_shape],
            [place],
            [kept, got, own_got, extra],
        )

        steps = list(range(0, blocks, 2))
        mine = [visit] + [across_blk(visit, k) for k in steps[1:]]
        near_block = across_blk(own_block, 1)
        mine = [visit] + [lax.optimization_barrier((v, own_block))[0] for v in mine[1:]]
        theirs = [lax.ppermute(v, "mp", SWAP) for v in mine]

        groups = [list(range(i, min(i + 2, len(steps)))) for i in range(0, len(steps), 2)]
        state = []
        for index, group in enumerate(groups):
            first, last = index == 0, index == len(groups) - 1
            pieces = [p for g in group for p in (mine[g], theirs[g])]
            if last:
                outs = [whole_f32, whole_b16, block_b16, loss_shape]
            else:
                outs = [
                    jax.ShapeDtypeStruct((2 * half, width), F32),
                    jax.ShapeDtypeStruct((2 * half, 1), F32),
                ]
            visited_rows = 2 * half * len(group)
            state = local_call(
                pair_kernel(len(group), first, last),
                "pairs",
                outs,
                [scale_bias],
                [own_block, near_block, own_ids, *pieces, *state],
                scratch=[
                    pltpu.VMEM((2 * half, width), BF16),
                    pltpu.VMEM((visited_rows, width), BF16),
                    pltpu.VMEM((8, visited_rows), F32),
                    pltpu.VMEM((EXTRA, LANES), F32),
                ],
                flops=8 * half * visited_rows * width,
                transcendentals=6 * half * visited_rows,
            )
        grad_keep, grad_own, grad_near, loss_own = state

        pairs = [(s, b) for s in range(sections) for b in range(blocks)]
        diagonal_pairs = [
            (s * blocks + b, (1 - s) * blocks + (b ^ 1)) for s, b in pairs
        ]
        diagonal = lax.ppermute(grad_near, ("sec", "blk"), diagonal_pairs)
        near = across_blk(grad_near, 1)
        across = lax.ppermute(grad_own, "sec", SWAP)
        demb, loss_mine = local_call(
            demb_kernel,
            "demb",
            [jax.ShapeDtypeStruct((2, half + EXTRA, width), BF16), loss_shape],
            [place],
            [
                grad_keep, near, across, diagonal,
                own_unit, own_norm, other_unit, other_norm, loss_own,
            ],
            scratch=[pltpu.VMEM((half, width), BF16), pltpu.VMEM((EXTRA, LANES), F32)],
        )
        demb_got = lax.ppermute(demb, "mp", SWAP)
        return local_call(
            grads_kernel,
            "grads",
            [
                jax.ShapeDtypeStruct((1, rows), F32),
                jax.ShapeDtypeStruct((rows, image_proj.shape[0]), BF16),
                jax.ShapeDtypeStruct((rows, text_proj.shape[0]), BF16),
            ],
            [place],
            [demb, demb_got, loss_mine, image_proj, text_proj],
            scratch=[pltpu.VMEM((rows, width), BF16)],
            flops=2 * embed_flops,
        )

    return per_device


def solution(mesh):
    placed = (
        P("blk", ("sec", "mp")),
        P("blk", ("sec", "mp")),
        P(("sec", "mp"), None),
        P(("sec", "mp"), None),
        P(),
        P(),
        P("blk"),
    )
    return jax.shard_map(
        make_per_device(mesh),
        mesh=mesh,
        in_specs=placed,
        out_specs=(P("sec", "blk"), P("blk", ("sec", "mp")), P("blk", ("sec", "mp"))),
        check_vma=False,
    )
```

```python
import jax
import jax.numpy as jnp
from jax import lax
from jax.experimental import pallas as pl
from jax.experimental.pallas import tpu as pltpu
from jax.sharding import PartitionSpec as P

F32 = jnp.float32
BF16 = jnp.bfloat16
SWAP = [(0, 1), (1, 0)]
NT = (((1,), (1,)), ((), ()))
VMEM_LIMIT = 16 * 1024 * 1024
LANES = 128
EXTRA = 8


def local_call(
    kernel, name, outs, arrays, scratch=(), flops=0, transcendentals=0, held=(),
):
    nbytes = sum(a.size * a.dtype.itemsize for a in (*arrays, *held))
    return pl.pallas_call(
        kernel,
        out_shape=outs,
        in_specs=[pl.BlockSpec(memory_space=pltpu.VMEM)] * len(arrays)
        + [pl.BlockSpec(memory_space=pltpu.HBM)] * len(held),
        out_specs=[pl.BlockSpec(memory_space=pltpu.VMEM)] * len(outs),
        scratch_shapes=list(scratch),
        compiler_params=pltpu.CompilerParams(vmem_limit_bytes=VMEM_LIMIT),
        cost_estimate=pl.CostEstimate(
            flops=flops, bytes_accessed=nbytes, transcendentals=transcendentals
        ),
        name=name,
    )(*arrays, *held)


def cuts(rows):
    size = 128 if rows % 128 == 0 else rows
    return [(start, size) for start in range(0, rows, size)]


def embed_rows(which, image_pooled, text_pooled, image_proj, text_proj, out, before):
    half = out.shape[1]
    core = lax.axis_index("mp")
    start = pl.multiple_of((core if which == 0 else 1 - core) * half, half)
    rows = pl.ds(start, half)
    for index, (pooled, proj) in enumerate(
        ((image_pooled, image_proj), (text_pooled, text_proj))
    ):
        for copy in before[index]:
            copy.wait()
        out[index] = jnp.dot(pooled[rows, :], proj[...], preferred_element_type=F32).astype(
            out.dtype
        )


def embed_sent_kernel(*refs):
    sources, sent, held, sems = refs[:4], refs[4], refs[5:9], refs[9]
    before = [[], []]
    count = 0
    for index in (0, 2, 1, 3):
        source, target = sources[index], held[index]
        for start, size in cuts(source.shape[0]):
            rows = pl.ds(start, size)
            copy = pltpu.make_async_copy(source.at[rows], target.at[rows], sems.at[count])
            copy.start()
            before[index % 2].append(copy)
            count += 1
    embed_rows(1, *held, sent, before)


def embed_kept_kernel(*refs):
    embed_rows(0, *refs[:4], refs[4], [[], []])


def join_cores_kernel(kept, got, own_send, other_send):
    section = lax.axis_index("sec")
    own_send[...] = (kept[section] + got[section].astype(F32)).astype(BF16)
    other_send[...] = (kept[1 - section] + got[1 - section].astype(F32)).astype(BF16)


def write_block(block, value, extra):
    half, width = value.shape
    for c in range(width // LANES):
        block[pl.ds(c * half, half), :] = value[:, c * LANES : (c + 1) * LANES].astype(BF16)
    block[pl.ds(half * (width // LANES), EXTRA), :] = extra.astype(BF16)


def read_block(block, target, start, half):
    for c in range(target.shape[1] // LANES):
        target[pl.ds(start, half), pl.ds(c * LANES, LANES)] = block[pl.ds(c * half, half), :]


def extra_rows(block):
    return block[pl.ds(block.shape[0] - EXTRA, EXTRA), :].astype(F32)


def block_ids(block):
    extra = extra_rows(block)
    return extra[0:1] * 128.0 + extra[1:2]


def split_rows(row, extra):
    high = row.astype(BF16).astype(F32)
    rest = row - high
    middle = rest.astype(BF16).astype(F32)
    extra[...] = jnp.zeros_like(extra)
    for index, part in enumerate((high, middle, rest - middle)):
        extra[index : index + 1, 0 : row.shape[1]] = part


def unit_kernel(own):
    def kernel(kept, got, summed, ids, unit, block, norm, extra):
        half = summed.shape[0]
        core = lax.axis_index("mp")
        half_ids = jnp.where(core == 0, ids[0:1, :half], ids[0:1, half : 2 * half])
        extra[...] = jnp.zeros_like(extra)
        extra[0:1, 0:half] = (half_ids >> 7).astype(F32)
        extra[1:2, 0:half] = (half_ids & 127).astype(F32)
        section = lax.axis_index("sec")
        section = section if own else 1 - section
        emb = kept[section] + got[section].astype(F32) + summed[...].astype(F32)
        row_norm = jnp.sqrt(jnp.sum(emb * emb, axis=1, keepdims=True) + 1e-06)
        value = emb / row_norm
        unit[...] = value
        norm[...] = row_norm
        write_block(block, value, extra[...])

    return kernel


def relay_kernel(block, out):
    out[...] = block[...]


def pair_kernel(blocks, first, last):
    def kernel(scale_bias, own_block, near_block, *refs):
        pieces = refs[: 2 * blocks]
        refs = refs[2 * blocks :]
        if not first:
            grad_in, loss_in = refs[:2]
            refs = refs[2:]
        if last:
            grad_keep, grad_own, grad_near, loss_own = refs[:4]
            refs = refs[4:]
        else:
            grad_out, loss_out = refs[:2]
            refs = refs[2:]
        own, visited, visit_ids, extra = refs
        half = own.shape[0] // 2
        read_block(own_block, own, 0, half)
        read_block(near_block, own, half, half)
        for index, piece in enumerate(pieces):
            read_block(piece, visited, index * half, half)
            visit_ids[0:1, pl.ds(index * half, half)] = block_ids(piece)[:, :half]
        ids = jnp.concatenate(
            [
                jnp.transpose(jnp.broadcast_to(block_ids(b), (LANES, LANES)))[:half, 0:1]
                for b in (own_block, near_block)
            ],
            axis=0,
        )
        scale = scale_bias[0:1, 0:1]
        scores = (
            scale * lax.dot_general(own[...], visited[...], NT, preferred_element_type=F32)
            + scale_bias[0:1, 1:2]
        )
        sign = jnp.where(ids == visit_ids[0:1, :], 1.0, -1.0).astype(F32)
        value = -sign * scores
        small = jnp.exp(-jnp.abs(value))
        losses = jnp.maximum(value, 0.0) + jnp.log1p(small)
        sigmoid = jnp.where(value >= 0.0, 1.0, small) / (1.0 + small)
        weight = (-scale * sign * sigmoid).astype(BF16)
        grad = jnp.dot(weight, visited[...], preferred_element_type=F32)
        loss = jnp.sum(losses, axis=1, keepdims=True)
        if not first:
            grad = grad + grad_in[...]
            loss = loss + loss_in[...]
        if last:
            grad_keep[...] = grad[:half]
            grad_own[...] = grad[:half].astype(BF16)
            wide = jnp.broadcast_to(loss, (2 * half, LANES))
            loss_own[...] = jnp.transpose(wide[:half])[0:1]
            split_rows(jnp.transpose(wide[half:])[0:1], extra)
            write_block(grad_near, grad[half:], extra[...])
        else:
            grad_out[...] = grad
            loss_out[...] = loss

    return kernel


def demb_kernel(
    kept, near, across, diagonal, own_unit, own_norm, other_unit, other_norm, loss_own,
    out, loss_mine, joined, extra,
):
    section = lax.axis_index("sec")
    half, width = own_unit.shape

    def finish(grad, unit, norm):
        value = unit[...]
        along = jnp.sum(value * grad, axis=1, keepdims=True)
        return ((grad - value * along) / norm[...]).astype(BF16)

    rows = pl.ds(0, half)
    read_block(diagonal, joined.at[0], 0, half)
    out[1 - section, rows, :] = finish(
        across[...].astype(F32) + joined[0].astype(F32), other_unit, other_norm
    )
    read_block(near, joined.at[1], 0, half)
    out[section, rows, :] = finish(kept[...] + joined[1].astype(F32), own_unit, own_norm)
    parts = extra_rows(near)
    loss = loss_own[...] + (parts[0:1] + parts[1:2] + parts[2:3])[:, :half]
    loss_mine[...] = loss
    split_rows(loss, extra)
    out[:, pl.ds(half, EXTRA), :] = jnp.zeros((2, EXTRA, width), BF16)
    out[0, pl.ds(half, EXTRA), pl.ds(0, LANES)] = extra[...].astype(BF16)


def grads_kernel(
    mine, theirs, loss_mine, image_proj, text_proj, pair_loss, image_grad, text_grad, joined
):
    half = joined.shape[1] // 2
    core = lax.axis_index("mp")
    for index, (proj, grad) in enumerate(((image_proj, image_grad), (text_proj, text_grad))):
        for spot, source in ((core, mine), (1 - core, theirs)):
            rows = pl.ds(pl.multiple_of(spot * half, half), half)
            joined[index, rows, :] = source[index, pl.ds(0, half), :]
        grad[...] = lax.dot_general(
            joined[index], proj[...], NT, preferred_element_type=F32
        ).astype(BF16)
    parts = theirs[0, pl.ds(half, EXTRA), pl.ds(0, LANES)].astype(F32)
    loss = loss_mine[...]
    loss_theirs = (parts[0:1] + parts[1:2] + parts[2:3])[:, :half]
    pair_loss[0:1, 0:half] = jnp.where(core == 0, loss, loss_theirs)
    pair_loss[0:1, half : 2 * half] = jnp.where(core == 0, loss_theirs, loss)


def make_per_device(mesh):
    sections = mesh.shape["sec"]
    blocks = mesh.shape["blk"]

    def across_blk(value, step):
        return lax.ppermute(value, "blk", [(i, i ^ step) for i in range(blocks)])

    def per_device(
        image_pooled, text_pooled, image_proj, text_proj, log_multiplier, logit_bias, ids
    ):
        scale_bias = jnp.concatenate([jnp.exp(log_multiplier), logit_bias])[None, :]
        rows = image_pooled.shape[0]
        half = rows // 2
        width = image_proj.shape[1]
        block_rows = half * (width // LANES) + EXTRA
        whole_f32 = jax.ShapeDtypeStruct((half, width), F32)
        whole_b16 = jax.ShapeDtypeStruct((half, width), BF16)
        block_b16 = jax.ShapeDtypeStruct((block_rows, LANES), BF16)
        norm_shape = jax.ShapeDtypeStruct((half, 1), F32)
        loss_shape = jax.ShapeDtypeStruct((1, half), F32)
        towers = (image_pooled, text_pooled, image_proj, text_proj)
        embed_flops = 2 * half * width * (image_proj.shape[0] + text_proj.shape[0])

        ids_row = ids[None, :]
        copies = sum(len(cuts(t.shape[0])) for t in towers)
        sent, *towers = local_call(
            embed_sent_kernel,
            "embed_sent",
            [jax.ShapeDtypeStruct((2, half, width), BF16)]
            + [jax.ShapeDtypeStruct(t.shape, t.dtype) for t in towers],
            [],
            scratch=[pltpu.SemaphoreType.DMA((copies,))],
            flops=embed_flops,
            held=[pltpu.with_memory_space_constraint(t, pltpu.HBM) for t in towers],
        )
        image_proj, text_proj = towers[2:]
        got = lax.ppermute(sent, "mp", SWAP)
        (kept,) = local_call(
            embed_kept_kernel,
            "embed_kept",
            [jax.ShapeDtypeStruct((2, half, width), F32)],
            towers,
            flops=embed_flops,
        )
        own_send, other_send = local_call(
            join_cores_kernel, "join_cores", [whole_b16, whole_b16], [kept, got]
        )
        other_got = lax.ppermute(own_send, "sec", SWAP)
        own_got = lax.ppermute(other_send, "sec", SWAP)
        other_unit, visit, other_norm = local_call(
            unit_kernel(False),
            "other_unit",
            [whole_f32, block_b16, norm_shape],
            [kept, got, other_got, ids_row],
            scratch=[pltpu.VMEM((EXTRA, LANES), F32)],
        )
        own_unit, own_block, own_norm = local_call(
            unit_kernel(True),
            "own_unit",
            [whole_f32, block_b16, norm_shape],
            [kept, got, own_got, ids_row],
            scratch=[pltpu.VMEM((EXTRA, LANES), F32)],
        )

        steps = list(range(0, blocks, 2))
        mine = [visit] + [across_blk(visit, k) for k in steps[1:]]
        near_block = across_blk(own_block, 1)
        mine = [visit] + [lax.optimization_barrier((v, own_block))[0] for v in mine[1:]]
        mine[-1:] = local_call(relay_kernel, "relay", [block_b16], [mine[-1]], flops=10**9)
        theirs = [lax.ppermute(v, "mp", SWAP) for v in mine]

        early = list(range(len(steps) - 1))
        groups = [early[i : i + 3] for i in range(0, len(early), 3)] + [[len(steps) - 1]]
        state = []
        for index, group in enumerate(groups):
            first, last = index == 0, index == len(groups) - 1
            pieces = [p for g in group for p in (mine[g], theirs[g])]
            if last:
                outs = [whole_f32, whole_b16, block_b16, loss_shape]
            else:
                outs = [
                    jax.ShapeDtypeStruct((2 * half, width), F32),
                    jax.ShapeDtypeStruct((2 * half, 1), F32),
                ]
            visited_rows = 2 * half * len(group)
            state = local_call(
                pair_kernel(len(group), first, last),
                "pairs",
                outs,
                [scale_bias, own_block, near_block, *pieces, *state],
                scratch=[
                    pltpu.VMEM((2 * half, width), BF16),
                    pltpu.VMEM((visited_rows, width), BF16),
                    pltpu.VMEM((8, visited_rows), F32),
                    pltpu.VMEM((EXTRA, LANES), F32),
                ],
                flops=8 * half * visited_rows * width,
                transcendentals=6 * half * visited_rows,
            )
        grad_keep, grad_own, grad_near, loss_own = state

        pairs = [(s, b) for s in range(sections) for b in range(blocks)]
        diagonal_pairs = [
            (s * blocks + b, (1 - s) * blocks + (b ^ 1)) for s, b in pairs
        ]
        diagonal = lax.ppermute(grad_near, ("sec", "blk"), diagonal_pairs)
        near = across_blk(grad_near, 1)
        across = lax.ppermute(grad_own, "sec", SWAP)
        demb, loss_mine = local_call(
            demb_kernel,
            "demb",
            [jax.ShapeDtypeStruct((2, half + EXTRA, width), BF16), loss_shape],
            [
                grad_keep, near, across, diagonal,
                own_unit, own_norm, other_unit, other_norm, loss_own,
            ],
            scratch=[pltpu.VMEM((2, half, width), BF16), pltpu.VMEM((EXTRA, LANES), F32)],
        )
        demb_got = lax.ppermute(demb, "mp", SWAP)
        return local_call(
            grads_kernel,
            "grads",
            [
                jax.ShapeDtypeStruct((1, rows), F32),
                jax.ShapeDtypeStruct((rows, image_proj.shape[0]), BF16),
                jax.ShapeDtypeStruct((rows, text_proj.shape[0]), BF16),
            ],
            [demb, demb_got, loss_mine, image_proj, text_proj],
            scratch=[pltpu.VMEM((2, rows, width), BF16)],
            flops=2 * embed_flops,
        )

    return per_device


def solution(mesh):
    placed = (
        P("blk", ("sec", "mp")),
        P("blk", ("sec", "mp")),
        P(("sec", "mp"), None),
        P(("sec", "mp"), None),
        P(),
        P(),
        P("blk"),
    )
    return jax.shard_map(
        make_per_device(mesh),
        mesh=mesh,
        in_specs=placed,
        out_specs=(P("sec", "blk"), P("blk", ("sec", "mp")), P("blk", ("sec", "mp"))),
        check_vma=False,
    )
```

```python
import jax
import jax.numpy as jnp
from jax import lax
from jax.experimental import pallas as pl
from jax.experimental.pallas import tpu as pltpu
from jax.sharding import PartitionSpec as P

F32 = jnp.float32
BF16 = jnp.bfloat16
SWAP = [(0, 1), (1, 0)]
NT = (((1,), (1,)), ((), ()))
VMEM_LIMIT = 16 * 1024 * 1024
LANES = 128
EXTRA = 8


def local_call(
    kernel, name, outs, arrays, scratch=(), flops=0, transcendentals=0, held=(),
):
    nbytes = sum(a.size * a.dtype.itemsize for a in (*arrays, *held))
    return pl.pallas_call(
        kernel,
        out_shape=outs,
        in_specs=[pl.BlockSpec(memory_space=pltpu.VMEM)] * len(arrays)
        + [pl.BlockSpec(memory_space=pltpu.HBM)] * len(held),
        out_specs=[pl.BlockSpec(memory_space=pltpu.VMEM)] * len(outs),
        scratch_shapes=list(scratch),
        compiler_params=pltpu.CompilerParams(vmem_limit_bytes=VMEM_LIMIT),
        cost_estimate=pl.CostEstimate(
            flops=flops, bytes_accessed=nbytes, transcendentals=transcendentals
        ),
        name=name,
    )(*arrays, *held)


def cuts(rows):
    size = 128 if rows % 128 == 0 else rows
    return [(start, size) for start in range(0, rows, size)]


def embed_rows(which, image_pooled, text_pooled, image_proj, text_proj, out, before):
    half = out.shape[1]
    core = lax.axis_index("mp")
    start = pl.multiple_of((core if which == 0 else 1 - core) * half, half)
    rows = pl.ds(start, half)
    for index, (pooled, proj) in enumerate(
        ((image_pooled, image_proj), (text_pooled, text_proj))
    ):
        for copy in before[index]:
            copy.wait()
        out[index] = jnp.dot(pooled[rows, :], proj[...], preferred_element_type=F32).astype(
            out.dtype
        )


def embed_sent_kernel(*refs):
    sources, sent, held, sems = refs[:4], refs[4], refs[5:9], refs[9]
    before = [[], []]
    count = 0
    for index in (0, 2, 1, 3):
        source, target = sources[index], held[index]
        for start, size in cuts(source.shape[0]):
            rows = pl.ds(start, size)
            copy = pltpu.make_async_copy(source.at[rows], target.at[rows], sems.at[count])
            copy.start()
            before[index % 2].append(copy)
            count += 1
    embed_rows(1, *held, sent, before)


def embed_kept_kernel(*refs):
    embed_rows(0, *refs[:4], refs[4], [[], []])


def join_cores_kernel(kept, got, own_send, other_send):
    section = lax.axis_index("sec")
    own_send[...] = (kept[section] + got[section].astype(F32)).astype(BF16)
    other_send[...] = (kept[1 - section] + got[1 - section].astype(F32)).astype(BF16)


def write_block(block, value, extra):
    half, width = value.shape
    for c in range(width // LANES):
        block[pl.ds(c * half, half), :] = value[:, c * LANES : (c + 1) * LANES].astype(BF16)
    block[pl.ds(half * (width // LANES), EXTRA), :] = extra.astype(BF16)


def read_block(block, target, start, half):
    for c in range(target.shape[1] // LANES):
        target[pl.ds(start, half), pl.ds(c * LANES, LANES)] = block[pl.ds(c * half, half), :]


def extra_rows(block):
    return block[pl.ds(block.shape[0] - EXTRA, EXTRA), :].astype(F32)


def block_ids(block):
    extra = extra_rows(block)
    return extra[0:1] * 128.0 + extra[1:2]


def split_rows(row, extra):
    high = row.astype(BF16).astype(F32)
    rest = row - high
    middle = rest.astype(BF16).astype(F32)
    extra[...] = jnp.zeros_like(extra)
    for index, part in enumerate((high, middle, rest - middle)):
        extra[index : index + 1, 0 : row.shape[1]] = part


def unit_kernel(own):
    def kernel(kept, got, summed, ids, *refs):
        if own:
            multiplier, bias, unit, block, norm, params, extra = refs
            params[0:1, :] = jnp.broadcast_to(jnp.exp(multiplier[...]), (1, LANES))
            params[1:2, :] = jnp.broadcast_to(bias[...], (1, LANES))
        else:
            unit, block, norm, extra = refs
        half = summed.shape[0]
        core = lax.axis_index("mp")
        half_ids = jnp.where(core == 0, ids[0:1, :half], ids[0:1, half : 2 * half])
        extra[...] = jnp.zeros_like(extra)
        extra[0:1, 0:half] = (half_ids >> 7).astype(F32)
        extra[1:2, 0:half] = (half_ids & 127).astype(F32)
        section = lax.axis_index("sec")
        section = section if own else 1 - section
        emb = kept[section] + got[section].astype(F32) + summed[...].astype(F32)
        row_norm = jnp.sqrt(jnp.sum(emb * emb, axis=1, keepdims=True) + 1e-06)
        value = emb / row_norm
        unit[...] = value
        norm[...] = row_norm
        write_block(block, value, extra[...])

    return kernel


def relay_kernel(block, out):
    out[...] = block[...]


def pair_kernel(blocks, sides, first, last):
    def kernel(params, *refs):
        sources, refs = refs[: len(sides)], refs[len(sides) :]
        pieces, refs = refs[: 2 * blocks], refs[2 * blocks :]
        if not first:
            (grad_in, loss_in), refs = refs[:2], refs[2:]
        outs, (own, visited, visit_ids, extra) = refs[:-4], refs[-4:]
        half = own.shape[0] // len(sides)
        columns = []
        for index, source in enumerate(sources):
            read_block(source, own, index * half, half)
            square = jnp.broadcast_to(block_ids(source), (LANES, LANES))
            columns.append(jnp.transpose(square)[:half, 0:1])
        ids = jnp.concatenate(columns, axis=0) if len(sides) > 1 else columns[0]
        for index, piece in enumerate(pieces):
            read_block(piece, visited, index * half, half)
            visit_ids[0:1, pl.ds(index * half, half)] = block_ids(piece)[:, :half]
        scale = params[0:1, 0:1]
        scores = (
            scale * lax.dot_general(own[...], visited[...], NT, preferred_element_type=F32)
            + params[1:2, 0:1]
        )
        sign = jnp.where(ids == visit_ids[0:1, :], 1.0, -1.0).astype(F32)
        value = -sign * scores
        small = jnp.exp(-jnp.abs(value))
        losses = jnp.maximum(value, 0.0) + jnp.log1p(small)
        sigmoid = jnp.where(value >= 0.0, 1.0, small) / (1.0 + small)
        weight = (-scale * sign * sigmoid).astype(BF16)
        grad = jnp.dot(weight, visited[...], preferred_element_type=F32)
        loss = jnp.sum(losses, axis=1, keepdims=True)
        if not first:
            rows = pl.ds(half * sides[0], half * len(sides))
            grad = grad + grad_in[rows, :]
            loss = loss + loss_in[rows, :]
        if not last:
            outs[0][...] = grad
            outs[1][...] = loss
            return
        loss_row = jnp.transpose(jnp.broadcast_to(loss, (half, LANES)))[0:1]
        if sides[0] == 0:
            grad_keep, grad_own, loss_own = outs
            grad_keep[...] = grad
            grad_own[...] = grad.astype(BF16)
            loss_own[...] = loss_row
        else:
            split_rows(loss_row, extra)
            write_block(outs[0], grad, extra[...])

    return kernel


def finish(grad, unit, norm):
    value = unit[...]
    along = jnp.sum(value * grad, axis=1, keepdims=True)
    return ((grad - value * along) / norm[...]).astype(BF16)


def own_demb_kernel(kept, near, unit, norm, loss_own, out, loss_mine, joined, extra):
    half, width = unit.shape
    read_block(near, joined, 0, half)
    out[pl.ds(0, half), :] = finish(kept[...] + joined[...].astype(F32), unit, norm)
    parts = extra_rows(near)
    loss = loss_own[...] + (parts[0:1] + parts[1:2] + parts[2:3])[:, :half]
    loss_mine[...] = loss
    split_rows(loss, extra)
    out[pl.ds(half, EXTRA), :] = jnp.zeros((EXTRA, width), BF16)
    out[pl.ds(half, EXTRA), pl.ds(0, LANES)] = extra[...].astype(BF16)


def other_demb_kernel(across, diagonal, unit, norm, out, joined):
    read_block(diagonal, joined, 0, unit.shape[0])
    out[...] = finish(across[...].astype(F32) + joined[...].astype(F32), unit, norm)


def grads_kernel(
    own, own_got, other, other_got, loss_mine, image_proj, text_proj,
    pair_loss, image_grad, text_grad, joined,
):
    half = joined.shape[1] // 2
    core = lax.axis_index("mp")

    def tower(index, mine, theirs, proj, grad):
        mine, theirs = mine[pl.ds(0, half), :], theirs[pl.ds(0, half), :]
        joined[index, pl.ds(0, half), :] = jnp.where(core == 0, mine, theirs)
        joined[index, pl.ds(half, half), :] = jnp.where(core == 0, theirs, mine)
        grad[...] = lax.dot_general(
            joined[index], proj[...], NT, preferred_element_type=F32
        ).astype(BF16)

    @pl.when(lax.axis_index("sec") == 0)
    def _():
        tower(0, own, own_got, image_proj, image_grad)
        tower(1, other, other_got, text_proj, text_grad)

    @pl.when(lax.axis_index("sec") != 0)
    def _():
        tower(1, own, own_got, text_proj, text_grad)
        tower(0, other, other_got, image_proj, image_grad)

    parts = own_got[pl.ds(half, EXTRA), pl.ds(0, LANES)].astype(F32)
    loss = loss_mine[...]
    loss_theirs = (parts[0:1] + parts[1:2] + parts[2:3])[:, :half]
    pair_loss[0:1, 0:half] = jnp.where(core == 0, loss, loss_theirs)
    pair_loss[0:1, half : 2 * half] = jnp.where(core == 0, loss_theirs, loss)


def make_per_device(mesh):
    sections = mesh.shape["sec"]
    blocks = mesh.shape["blk"]

    def across_blk(value, step):
        return lax.ppermute(value, "blk", [(i, i ^ step) for i in range(blocks)])

    def per_device(
        image_pooled, text_pooled, image_proj, text_proj, log_multiplier, logit_bias, ids
    ):
        multiplier, bias = log_multiplier[None, :], logit_bias[None, :]
        rows = image_pooled.shape[0]
        half = rows // 2
        width = image_proj.shape[1]
        block_rows = half * (width // LANES) + EXTRA
        whole_f32 = jax.ShapeDtypeStruct((half, width), F32)
        whole_b16 = jax.ShapeDtypeStruct((half, width), BF16)
        block_b16 = jax.ShapeDtypeStruct((block_rows, LANES), BF16)
        norm_shape = jax.ShapeDtypeStruct((half, 1), F32)
        loss_shape = jax.ShapeDtypeStruct((1, half), F32)
        towers = (image_pooled, text_pooled, image_proj, text_proj)
        embed_flops = 2 * half * width * (image_proj.shape[0] + text_proj.shape[0])

        ids_row = ids[None, :]
        copies = sum(len(cuts(t.shape[0])) for t in towers)
        sent, *towers = local_call(
            embed_sent_kernel,
            "embed_sent",
            [jax.ShapeDtypeStruct((2, half, width), BF16)]
            + [jax.ShapeDtypeStruct(t.shape, t.dtype) for t in towers],
            [],
            scratch=[pltpu.SemaphoreType.DMA((copies,))],
            flops=embed_flops,
            held=[pltpu.with_memory_space_constraint(t, pltpu.HBM) for t in towers],
        )
        image_proj, text_proj = towers[2:]
        got = lax.ppermute(sent, "mp", SWAP)
        (kept,) = local_call(
            embed_kept_kernel,
            "embed_kept",
            [jax.ShapeDtypeStruct((2, half, width), F32)],
            towers,
            flops=embed_flops,
        )
        own_send, other_send = local_call(
            join_cores_kernel, "join_cores", [whole_b16, whole_b16], [kept, got]
        )
        other_got = lax.ppermute(own_send, "sec", SWAP)
        own_got = lax.ppermute(other_send, "sec", SWAP)
        other_unit, visit, other_norm = local_call(
            unit_kernel(False),
            "other_unit",
            [whole_f32, block_b16, norm_shape],
            [kept, got, other_got, ids_row],
            scratch=[pltpu.VMEM((EXTRA, LANES), F32)],
        )
        own_unit, own_block, own_norm, params = local_call(
            unit_kernel(True),
            "own_unit",
            [whole_f32, block_b16, norm_shape, jax.ShapeDtypeStruct((2, LANES), F32)],
            [kept, got, own_got, ids_row, multiplier, bias],
            scratch=[pltpu.VMEM((EXTRA, LANES), F32)],
        )

        steps = list(range(0, blocks, 2))
        mine = [visit] + [across_blk(visit, k) for k in steps[1:]]
        near_block = across_blk(own_block, 1)
        mine = [visit] + [lax.optimization_barrier((v, own_block))[0] for v in mine[1:]]
        mine[-1:] = local_call(relay_kernel, "relay", [block_b16], [mine[-1]], flops=10**9)
        theirs = [lax.ppermute(v, "mp", SWAP) for v in mine]

        early = list(range(len(steps) - 1))
        groups = [early[i : i + 3] for i in range(0, len(early), 3)] + [[len(steps) - 1]]
        state = []
        for index, group in enumerate(groups):
            first, last = index == 0, index == len(groups) - 1
            pieces = [p for g in group for p in (mine[g], theirs[g])]
            visited_rows = 2 * half * len(group)

            def score(sides, outs):
                sources = [(own_block, near_block)[side] for side in sides]
                return local_call(
                    pair_kernel(len(group), sides, first, last),
                    "pairs",
                    outs,
                    [params, *sources, *pieces, *state],
                    scratch=[
                        pltpu.VMEM((len(sides) * half, width), BF16),
                        pltpu.VMEM((visited_rows, width), BF16),
                        pltpu.VMEM((8, visited_rows), F32),
                        pltpu.VMEM((EXTRA, LANES), F32),
                    ],
                    flops=4 * len(sides) * half * visited_rows * width,
                    transcendentals=3 * len(sides) * half * visited_rows,
                )

            if last:
                grad_keep, grad_own, loss_own = score((0,), [whole_f32, whole_b16, loss_shape])
                (grad_near,) = score((1,), [block_b16])
            else:
                state = score(
                    (0, 1),
                    [
                        jax.ShapeDtypeStruct((2 * half, width), F32),
                        jax.ShapeDtypeStruct((2 * half, 1), F32),
                    ],
                )

        pairs = [(s, b) for s in range(sections) for b in range(blocks)]
        diagonal_pairs = [
            (s * blocks + b, (1 - s) * blocks + (b ^ 1)) for s, b in pairs
        ]
        diagonal = lax.ppermute(grad_near, ("sec", "blk"), diagonal_pairs)
        near = across_blk(grad_near, 1)
        across = lax.ppermute(grad_own, "sec", SWAP)
        own_demb, loss_mine = local_call(
            own_demb_kernel,
            "own_demb",
            [jax.ShapeDtypeStruct((half + EXTRA, width), BF16), loss_shape],
            [grad_keep, near, own_unit, own_norm, loss_own],
            scratch=[pltpu.VMEM((half, width), BF16), pltpu.VMEM((EXTRA, LANES), F32)],
        )
        own_got = lax.ppermute(own_demb, "mp", SWAP)
        (other_demb,) = local_call(
            other_demb_kernel,
            "other_demb",
            [whole_b16],
            [across, diagonal, other_unit, other_norm],
            scratch=[pltpu.VMEM((half, width), BF16)],
        )
        other_got = lax.ppermute(other_demb, "mp", SWAP)
        return local_call(
            grads_kernel,
            "grads",
            [
                jax.ShapeDtypeStruct((1, rows), F32),
                jax.ShapeDtypeStruct((rows, image_proj.shape[0]), BF16),
                jax.ShapeDtypeStruct((rows, text_proj.shape[0]), BF16),
            ],
            [own_demb, own_got, other_demb, other_got, loss_mine, image_proj, text_proj],
            scratch=[pltpu.VMEM((2, rows, width), BF16)],
            flops=2 * embed_flops,
        )

    return per_device


def solution(mesh):
    placed = (
        P("blk", ("sec", "mp")),
        P("blk", ("sec", "mp")),
        P(("sec", "mp"), None),
        P(("sec", "mp"), None),
        P(),
        P(),
        P("blk"),
    )
    return jax.shard_map(
        make_per_device(mesh),
        mesh=mesh,
        in_specs=placed,
        out_specs=(P("sec", "blk"), P("blk", ("sec", "mp")), P("blk", ("sec", "mp"))),
        check_vma=False,
    )
```

```python
import jax
import jax.numpy as jnp
from jax import lax
from jax.experimental import pallas as pl
from jax.experimental.pallas import tpu as pltpu
from jax.sharding import PartitionSpec as P

F32 = jnp.float32
BF16 = jnp.bfloat16
SWAP = [(0, 1), (1, 0)]
NT = (((1,), (1,)), ((), ()))
VMEM_LIMIT = 16 * 1024 * 1024
LANES = 128
EXTRA = 8


def local_call(
    kernel, name, outs, arrays, scratch=(), flops=0, transcendentals=0, held=(),
):
    nbytes = sum(a.size * a.dtype.itemsize for a in (*arrays, *held))
    return pl.pallas_call(
        kernel,
        out_shape=outs,
        in_specs=[pl.BlockSpec(memory_space=pltpu.VMEM)] * len(arrays)
        + [pl.BlockSpec(memory_space=pltpu.HBM)] * len(held),
        out_specs=[pl.BlockSpec(memory_space=pltpu.VMEM)] * len(outs),
        scratch_shapes=list(scratch),
        compiler_params=pltpu.CompilerParams(vmem_limit_bytes=VMEM_LIMIT),
        cost_estimate=pl.CostEstimate(
            flops=flops, bytes_accessed=nbytes, transcendentals=transcendentals
        ),
        name=name,
    )(*arrays, *held)


def cuts(rows):
    size = 128 if rows % 128 == 0 else rows
    return [(start, size) for start in range(0, rows, size)]


def embed_rows(which, image_pooled, text_pooled, image_proj, text_proj, out, before):
    half = out.shape[1]
    core = lax.axis_index("mp")
    start = pl.multiple_of((core if which == 0 else 1 - core) * half, half)
    rows = pl.ds(start, half)
    for index, (pooled, proj) in enumerate(
        ((image_pooled, image_proj), (text_pooled, text_proj))
    ):
        for copy in before[index]:
            copy.wait()
        out[index] = jnp.dot(pooled[rows, :], proj[...], preferred_element_type=F32).astype(
            out.dtype
        )


def embed_sent_kernel(*refs):
    sources, sent, held, sems = refs[:4], refs[4], refs[5:9], refs[9]
    before = [[], []]
    count = 0
    for index in (0, 2, 1, 3):
        source, target = sources[index], held[index]
        for start, size in cuts(source.shape[0]):
            rows = pl.ds(start, size)
            copy = pltpu.make_async_copy(source.at[rows], target.at[rows], sems.at[count])
            copy.start()
            before[index % 2].append(copy)
            count += 1
    embed_rows(1, *held, sent, before)


def embed_kept_kernel(*refs):
    embed_rows(0, *refs[:4], refs[4], [[], []])


def join_cores_kernel(kept, got, own_send, other_send):
    section = lax.axis_index("sec")
    own_send[...] = (kept[section] + got[section].astype(F32)).astype(BF16)
    other_send[...] = (kept[1 - section] + got[1 - section].astype(F32)).astype(BF16)


def block_rows(half, width):
    return half * (width // LANES) + EXTRA


def write_block(block, value, extra, base=0):
    half, width = value.shape
    for c in range(width // LANES):
        rows = pl.ds(base + c * half, half)
        block[rows, :] = value[:, c * LANES : (c + 1) * LANES].astype(BF16)
    block[pl.ds(base + half * (width // LANES), EXTRA), :] = extra.astype(BF16)


def read_block(block, target, start, half, base=0):
    for c in range(target.shape[1] // LANES):
        rows = pl.ds(base + c * half, half)
        target[pl.ds(start, half), pl.ds(c * LANES, LANES)] = block[rows, :]


def extra_rows(block, end=None):
    end = block.shape[0] if end is None else end
    return block[pl.ds(end - EXTRA, EXTRA), :].astype(F32)


def block_ids(block, end=None):
    extra = extra_rows(block, end)
    return extra[0:1] * 128.0 + extra[1:2]


def split_rows(row, extra):
    high = row.astype(BF16).astype(F32)
    rest = row - high
    middle = rest.astype(BF16).astype(F32)
    extra[...] = jnp.zeros_like(extra)
    for index, part in enumerate((high, middle, rest - middle)):
        extra[index : index + 1, 0 : row.shape[1]] = part


def unit_kernel(own):
    def kernel(kept, got, summed, ids, *refs):
        if own:
            multiplier, bias, unit, block, norm, params, extra = refs
            params[0:1, :] = jnp.broadcast_to(jnp.exp(multiplier[...]), (1, LANES))
            params[1:2, :] = jnp.broadcast_to(bias[...], (1, LANES))
        else:
            unit, block, norm, extra = refs
        half, width = summed.shape
        core = lax.axis_index("mp")
        section = lax.axis_index("sec")
        section = section if own else 1 - section
        emb = kept[section] + got[section].astype(F32) + summed[...].astype(F32)
        row_norm = jnp.sqrt(jnp.sum(emb * emb, axis=1, keepdims=True) + 1e-06)
        value = emb / row_norm
        unit[...] = value
        norm[...] = row_norm
        half_ids = jnp.where(core == 0, ids[0:1, :half], ids[0:1, half : 2 * half])
        size = half if own else half // 2
        for index, start in enumerate(range(0, half, size)):
            some = half_ids[:, start : start + size]
            extra[index] = jnp.zeros_like(extra[index])
            extra[index, 0:1, 0:size] = (some >> 7).astype(F32)
            extra[index, 1:2, 0:size] = (some & 127).astype(F32)
            base = index * block_rows(size, width)
            write_block(block, value[start : start + size], extra[index], base)

    return kernel


def join_far_kernel(parts):
    def kernel(*refs):
        size = refs[0].shape[0]
        out = refs[-1]
        if parts == 1:
            out[...] = refs[0][...]
            return
        inner, first, direct, passed = lax.axis_index("blk"), refs[0], refs[1], refs[2]
        inner = jnp.logical_and(inner >= 2, inner < 6)
        out[pl.ds(0, size), :] = first[...]
        out[pl.ds(size, size), :] = jnp.where(inner, direct[...], passed[...])

    return kernel


def pair_kernel(blocks, sides, first, last):
    def kernel(params, *refs):
        sources, refs = refs[: len(sides)], refs[len(sides) :]
        pieces, refs = refs[:blocks], refs[blocks:]
        if not first:
            (grad_in, loss_in), refs = refs[:2], refs[2:]
        outs, (own, visited, visit_ids, extra) = refs[:-4], refs[-4:]
        half = own.shape[0] // len(sides)
        columns = []
        for index, source in enumerate(sources):
            read_block(source, own, index * half, half)
            square = jnp.broadcast_to(block_ids(source), (LANES, LANES))
            columns.append(jnp.transpose(square)[:half, 0:1])
        ids = jnp.concatenate(columns, axis=0) if len(sides) > 1 else columns[0]
        part = half // 2
        size = block_rows(part, own.shape[1])
        start = 0
        for piece in pieces:
            for base in range(0, piece.shape[0], size):
                read_block(piece, visited, start, part, base)
                ids_row = block_ids(piece, base + size)
                visit_ids[0:1, pl.ds(start, part)] = ids_row[:, :part]
                start += part
        scale = params[0:1, 0:1]
        scores = (
            scale * lax.dot_general(own[...], visited[...], NT, preferred_element_type=F32)
            + params[1:2, 0:1]
        )
        sign = jnp.where(ids == visit_ids[0:1, :], 1.0, -1.0).astype(F32)
        value = -sign * scores
        small = jnp.exp(-jnp.abs(value))
        losses = jnp.maximum(value, 0.0) + jnp.log1p(small)
        sigmoid = jnp.where(value >= 0.0, 1.0, small) / (1.0 + small)
        weight = (-scale * sign * sigmoid).astype(BF16)
        grad = jnp.dot(weight, visited[...], preferred_element_type=F32)
        loss = jnp.sum(losses, axis=1, keepdims=True)
        if not first:
            rows = pl.ds(half * sides[0], half * len(sides))
            grad = grad + grad_in[rows, :]
            loss = loss + loss_in[rows, :]
        if not last:
            outs[0][...] = grad
            outs[1][...] = loss
            return
        loss_row = jnp.transpose(jnp.broadcast_to(loss, (half, LANES)))[0:1]
        if sides[0] == 0:
            grad_keep, grad_own, loss_own = outs
            grad_keep[...] = grad
            grad_own[...] = grad.astype(BF16)
            loss_own[...] = loss_row
        else:
            split_rows(loss_row, extra)
            write_block(outs[0], grad, extra[...])

    return kernel


def finish(grad, unit, norm):
    value = unit[...]
    along = jnp.sum(value * grad, axis=1, keepdims=True)
    return ((grad - value * along) / norm[...]).astype(BF16)


def own_demb_kernel(kept, near, unit, norm, loss_own, out, loss_mine, joined, extra):
    half, width = unit.shape
    read_block(near, joined, 0, half)
    out[pl.ds(0, half), :] = finish(kept[...] + joined[...].astype(F32), unit, norm)
    parts = extra_rows(near)
    loss = loss_own[...] + (parts[0:1] + parts[1:2] + parts[2:3])[:, :half]
    loss_mine[...] = loss
    split_rows(loss, extra)
    out[pl.ds(half, EXTRA), :] = jnp.zeros((EXTRA, width), BF16)
    out[pl.ds(half, EXTRA), pl.ds(0, LANES)] = extra[...].astype(BF16)


def other_demb_kernel(across, diagonal, unit, norm, out, joined):
    read_block(diagonal, joined, 0, unit.shape[0])
    out[...] = finish(across[...].astype(F32) + joined[...].astype(F32), unit, norm)


def grads_kernel(
    own, own_got, other, other_got, loss_mine, image_proj, text_proj,
    pair_loss, image_grad, text_grad, joined,
):
    half = joined.shape[1] // 2
    core = lax.axis_index("mp")

    def tower(index, mine, theirs, proj, grad):
        mine, theirs = mine[pl.ds(0, half), :], theirs[pl.ds(0, half), :]
        joined[index, pl.ds(0, half), :] = jnp.where(core == 0, mine, theirs)
        joined[index, pl.ds(half, half), :] = jnp.where(core == 0, theirs, mine)
        grad[...] = lax.dot_general(
            joined[index], proj[...], NT, preferred_element_type=F32
        ).astype(BF16)

    @pl.when(lax.axis_index("sec") == 0)
    def _():
        tower(0, own, own_got, image_proj, image_grad)
        tower(1, other, other_got, text_proj, text_grad)

    @pl.when(lax.axis_index("sec") != 0)
    def _():
        tower(1, own, own_got, text_proj, text_grad)
        tower(0, other, other_got, image_proj, image_grad)

    parts = own_got[pl.ds(half, EXTRA), pl.ds(0, LANES)].astype(F32)
    loss = loss_mine[...]
    loss_theirs = (parts[0:1] + parts[1:2] + parts[2:3])[:, :half]
    pair_loss[0:1, 0:half] = jnp.where(core == 0, loss, loss_theirs)
    pair_loss[0:1, half : 2 * half] = jnp.where(core == 0, loss_theirs, loss)


def make_per_device(mesh):
    sections = mesh.shape["sec"]
    blocks = mesh.shape["blk"]

    def across_blk(value, step):
        return lax.ppermute(value, "blk", [(i, i ^ step) for i in range(blocks)])

    def per_device(
        image_pooled, text_pooled, image_proj, text_proj, log_multiplier, logit_bias, ids
    ):
        multiplier, bias = log_multiplier[None, :], logit_bias[None, :]
        rows = image_pooled.shape[0]
        half = rows // 2
        width = image_proj.shape[1]
        part_rows = block_rows(half // 2, width)
        whole_f32 = jax.ShapeDtypeStruct((half, width), F32)
        whole_b16 = jax.ShapeDtypeStruct((half, width), BF16)
        block_b16 = jax.ShapeDtypeStruct((block_rows(half, width), LANES), BF16)
        visit_b16 = jax.ShapeDtypeStruct((2 * part_rows, LANES), BF16)
        norm_shape = jax.ShapeDtypeStruct((half, 1), F32)
        loss_shape = jax.ShapeDtypeStruct((1, half), F32)
        towers = (image_pooled, text_pooled, image_proj, text_proj)
        embed_flops = 2 * half * width * (image_proj.shape[0] + text_proj.shape[0])

        ids_row = ids[None, :]
        copies = sum(len(cuts(t.shape[0])) for t in towers)
        sent, *towers = local_call(
            embed_sent_kernel,
            "embed_sent",
            [jax.ShapeDtypeStruct((2, half, width), BF16)]
            + [jax.ShapeDtypeStruct(t.shape, t.dtype) for t in towers],
            [],
            scratch=[pltpu.SemaphoreType.DMA((copies,))],
            flops=embed_flops,
            held=[pltpu.with_memory_space_constraint(t, pltpu.HBM) for t in towers],
        )
        image_proj, text_proj = towers[2:]
        got = lax.ppermute(sent, "mp", SWAP)
        (kept,) = local_call(
            embed_kept_kernel,
            "embed_kept",
            [jax.ShapeDtypeStruct((2, half, width), F32)],
            towers,
            flops=embed_flops,
        )
        own_send, other_send = local_call(
            join_cores_kernel, "join_cores", [whole_b16, whole_b16], [kept, got]
        )
        other_got = lax.ppermute(own_send, "sec", SWAP)
        own_got = lax.ppermute(other_send, "sec", SWAP)
        other_unit, visit, other_norm = local_call(
            unit_kernel(False),
            "other_unit",
            [whole_f32, visit_b16, norm_shape],
            [kept, got, other_got, ids_row],
            scratch=[pltpu.VMEM((2, EXTRA, LANES), F32)],
        )
        own_unit, own_block, own_norm, params = local_call(
            unit_kernel(True),
            "own_unit",
            [whole_f32, block_b16, norm_shape, jax.ShapeDtypeStruct((2, LANES), F32)],
            [kept, got, own_got, ids_row, multiplier, bias],
            scratch=[pltpu.VMEM((1, EXTRA, LANES), F32)],
        )

        steps = list(range(0, blocks, 2))
        mine = [across_blk(visit, k) for k in steps[1:-1]]
        if blocks == 8:
            first = across_blk(visit[:part_rows], 6)
            second = visit[part_rows:]
            direct = lax.ppermute(second, "blk", [(2, 4), (4, 2), (3, 5), (5, 3)])
            passed = mine[1][part_rows:]
            passed = lax.ppermute(passed, "blk", [(4, 6), (5, 7), (2, 0), (3, 1)])
            far = [first, direct, passed]
        else:
            far = [across_blk(visit, steps[-1])]
        near_block = across_blk(own_block, 1)
        mine = [lax.optimization_barrier((v, own_block))[0] for v in mine]
        far = [lax.optimization_barrier((v, own_block))[0] for v in far]
        mine = [visit, *mine]
        mine += local_call(join_far_kernel(len(far)), "join_far", [visit_b16], far, flops=10**9)
        theirs = [lax.ppermute(v, "mp", SWAP) for v in mine]

        early = list(range(len(steps) - 1))
        groups = [early[i : i + 3] for i in range(0, len(early), 3)] + [[len(steps) - 1]]
        state = []
        for index, group in enumerate(groups):
            first, last = index == 0, index == len(groups) - 1
            pieces = [p for g in group for p in (mine[g], theirs[g])]
            visited_rows = 2 * half * len(group)

            def score(sides, outs):
                sources = [(own_block, near_block)[side] for side in sides]
                return local_call(
                    pair_kernel(len(pieces), sides, first, last),
                    "pairs",
                    outs,
                    [params, *sources, *pieces, *state],
                    scratch=[
                        pltpu.VMEM((len(sides) * half, width), BF16),
                        pltpu.VMEM((visited_rows, width), BF16),
                        pltpu.VMEM((8, visited_rows), F32),
                        pltpu.VMEM((EXTRA, LANES), F32),
                    ],
                    flops=4 * len(sides) * half * visited_rows * width,
                    transcendentals=3 * len(sides) * half * visited_rows,
                )

            if last:
                grad_keep, grad_own, loss_own = score((0,), [whole_f32, whole_b16, loss_shape])
                (grad_near,) = score((1,), [block_b16])
            else:
                state = score(
                    (0, 1),
                    [
                        jax.ShapeDtypeStruct((2 * half, width), F32),
                        jax.ShapeDtypeStruct((2 * half, 1), F32),
                    ],
                )

        pairs = [(s, b) for s in range(sections) for b in range(blocks)]
        diagonal_pairs = [
            (s * blocks + b, (1 - s) * blocks + (b ^ 1)) for s, b in pairs
        ]
        diagonal = lax.ppermute(grad_near, ("sec", "blk"), diagonal_pairs)
        near = across_blk(grad_near, 1)
        across = lax.ppermute(grad_own, "sec", SWAP)
        own_demb, loss_mine = local_call(
            own_demb_kernel,
            "own_demb",
            [jax.ShapeDtypeStruct((half + EXTRA, width), BF16), loss_shape],
            [grad_keep, near, own_unit, own_norm, loss_own],
            scratch=[pltpu.VMEM((half, width), BF16), pltpu.VMEM((EXTRA, LANES), F32)],
        )
        own_got = lax.ppermute(own_demb, "mp", SWAP)
        (other_demb,) = local_call(
            other_demb_kernel,
            "other_demb",
            [whole_b16],
            [across, diagonal, other_unit, other_norm],
            scratch=[pltpu.VMEM((half, width), BF16)],
        )
        other_got = lax.ppermute(other_demb, "mp", SWAP)
        return local_call(
            grads_kernel,
            "grads",
            [
                jax.ShapeDtypeStruct((1, rows), F32),
                jax.ShapeDtypeStruct((rows, image_proj.shape[0]), BF16),
                jax.ShapeDtypeStruct((rows, text_proj.shape[0]), BF16),
            ],
            [own_demb, own_got, other_demb, other_got, loss_mine, image_proj, text_proj],
            scratch=[pltpu.VMEM((2, rows, width), BF16)],
            flops=2 * embed_flops,
        )

    return per_device


def solution(mesh):
    placed = (
        P("blk", ("sec", "mp")),
        P("blk", ("sec", "mp")),
        P(("sec", "mp"), None),
        P(("sec", "mp"), None),
        P(),
        P(),
        P("blk"),
    )
    return jax.shard_map(
        make_per_device(mesh),
        mesh=mesh,
        in_specs=placed,
        out_specs=(P("sec", "blk"), P("blk", ("sec", "mp")), P("blk", ("sec", "mp"))),
        check_vma=False,
    )
```

```python
import jax
import jax.numpy as jnp
from jax import lax
from jax.experimental import pallas as pl
from jax.experimental.pallas import tpu as pltpu
from jax.sharding import PartitionSpec as P

F32 = jnp.float32
BF16 = jnp.bfloat16
SWAP = [(0, 1), (1, 0)]
NT = (((1,), (1,)), ((), ()))
VMEM_LIMIT = 16 * 1024 * 1024
LANES = 128
EXTRA = 8


def local_call(
    kernel, name, outs, arrays, scratch=(), flops=0, transcendentals=0, held=(),
    aliases=(),
):
    nbytes = sum(a.size * a.dtype.itemsize for a in (*arrays, *held))
    return pl.pallas_call(
        kernel,
        out_shape=outs,
        in_specs=[pl.BlockSpec(memory_space=pltpu.VMEM)] * len(arrays)
        + [pl.BlockSpec(memory_space=pltpu.HBM)] * len(held),
        out_specs=[pl.BlockSpec(memory_space=pltpu.VMEM)] * len(outs),
        scratch_shapes=list(scratch),
        compiler_params=pltpu.CompilerParams(vmem_limit_bytes=VMEM_LIMIT),
        cost_estimate=pl.CostEstimate(
            flops=flops, bytes_accessed=nbytes, transcendentals=transcendentals
        ),
        name=name,
        input_output_aliases=dict(aliases),
    )(*arrays, *held)


def cuts(rows):
    size = 128 if rows % 128 == 0 else rows
    return [(start, size) for start in range(0, rows, size)]


def own_first(image, text, own, body):
    is_image = (lax.axis_index("sec") == 0) == own
    pl.when(is_image)(lambda: body(*image))
    pl.when(jnp.logical_not(is_image))(lambda: body(*text))


def bring(sources, targets, sems):
    copies = []
    for source, target in zip(sources, targets):
        for start, size in cuts(source.shape[0]):
            rows = pl.ds(start, size)
            sem = sems.at[len(copies)]
            copies.append(pltpu.make_async_copy(source.at[rows], target.at[rows], sem))
            copies[-1].start()
    return copies


def embed(pooled, proj, out, keep):
    half = out.shape[0]
    core = lax.axis_index("mp")
    rows = pl.ds(pl.multiple_of((core if keep else 1 - core) * half, half), half)
    out[...] = jnp.dot(pooled[rows, :], proj[...], preferred_element_type=F32).astype(out.dtype)


def own_sent_kernel(
    image_pooled, text_pooled, image_proj, text_proj,
    sent, image_rows, text_rows, image_held, text_held, sems,
):
    def body(pooled, proj, rows, held):
        for copy in bring((pooled, proj), (rows, held), sems):
            copy.wait()
        embed(rows, held, sent, False)

    image = (image_pooled, image_proj, image_rows, image_held)
    own_first(image, (text_pooled, text_proj, text_rows, text_held), True, body)


def own_kept_kernel(image_rows, text_rows, image_held, text_held, kept):
    own_first(
        (image_rows, image_held),
        (text_rows, text_held),
        True,
        lambda rows, held: embed(rows, held, kept, True),
    )


def other_embed_kernel(
    image_rows_in, text_rows_in, image_held_in, text_held_in, _,
    image_pooled, text_pooled, image_proj, text_proj,
    sent, kept, image_held, text_held, image_rows, text_rows, sems,
):
    def body(pooled, proj, rows, held):
        for copy in bring((pooled, proj), (rows, held), sems):
            copy.wait()
        embed(rows, held, sent, False)
        embed(rows, held, kept, True)

    image = (image_pooled, image_proj, image_rows, image_held)
    own_first(image, (text_pooled, text_proj, text_rows, text_held), False, body)


def join_cores_kernel(kept, got, send):
    send[...] = (kept[...] + got[...].astype(F32)).astype(BF16)


def write_block(block, value, extra):
    half, width = value.shape
    for c in range(width // LANES):
        block[pl.ds(c * half, half), :] = value[:, c * LANES : (c + 1) * LANES].astype(BF16)
    block[pl.ds(half * (width // LANES), EXTRA), :] = extra.astype(BF16)


def read_block(block, target, start, half):
    for c in range(target.shape[1] // LANES):
        target[pl.ds(start, half), pl.ds(c * LANES, LANES)] = block[pl.ds(c * half, half), :]


def extra_rows(block):
    return block[pl.ds(block.shape[0] - EXTRA, EXTRA), :].astype(F32)


def block_ids(block):
    extra = extra_rows(block)
    return extra[0:1] * 128.0 + extra[1:2]


def split_rows(row, extra):
    high = row.astype(BF16).astype(F32)
    rest = row - high
    middle = rest.astype(BF16).astype(F32)
    extra[...] = jnp.zeros_like(extra)
    for index, part in enumerate((high, middle, rest - middle)):
        extra[index : index + 1, 0 : row.shape[1]] = part


def unit_kernel(own):
    def kernel(kept, got, summed, ids, *refs):
        if own:
            multiplier, bias, unit, block, norm, params, extra = refs
            params[0:1, :] = jnp.broadcast_to(jnp.exp(multiplier[...]), (1, LANES))
            params[1:2, :] = jnp.broadcast_to(bias[...], (1, LANES))
        else:
            unit, block, norm, extra = refs
        half = summed.shape[0]
        core = lax.axis_index("mp")
        half_ids = jnp.where(core == 0, ids[0:1, :half], ids[0:1, half : 2 * half])
        extra[...] = jnp.zeros_like(extra)
        extra[0:1, 0:half] = (half_ids >> 7).astype(F32)
        extra[1:2, 0:half] = (half_ids & 127).astype(F32)
        emb = kept[...] + got[...].astype(F32) + summed[...].astype(F32)
        row_norm = jnp.sqrt(jnp.sum(emb * emb, axis=1, keepdims=True) + 1e-06)
        value = emb / row_norm
        unit[...] = value
        norm[...] = row_norm
        write_block(block, value, extra[...])

    return kernel


def relay_kernel(block, out):
    out[...] = block[...]


def pair_kernel(blocks, sides, first, last):
    def kernel(params, *refs):
        sources, refs = refs[: len(sides)], refs[len(sides) :]
        pieces, refs = refs[: 2 * blocks], refs[2 * blocks :]
        if not first:
            (grad_in, loss_in), refs = refs[:2], refs[2:]
        outs, (own, visited, visit_ids, extra) = refs[:-4], refs[-4:]
        half = own.shape[0] // len(sides)
        columns = []
        for index, source in enumerate(sources):
            read_block(source, own, index * half, half)
            square = jnp.broadcast_to(block_ids(source), (LANES, LANES))
            columns.append(jnp.transpose(square)[:half, 0:1])
        ids = jnp.concatenate(columns, axis=0) if len(sides) > 1 else columns[0]
        for index, piece in enumerate(pieces):
            read_block(piece, visited, index * half, half)
            visit_ids[0:1, pl.ds(index * half, half)] = block_ids(piece)[:, :half]
        scale = params[0:1, 0:1]
        scores = (
            scale * lax.dot_general(own[...], visited[...], NT, preferred_element_type=F32)
            + params[1:2, 0:1]
        )
        match = ids == visit_ids[0:1, :]
        value = jnp.where(match, -scores, scores)
        small = jnp.exp(-jnp.abs(value))
        total = 1.0 + small
        losses = jnp.maximum(value, 0.0) + jnp.log(total)
        sigmoid = jnp.where(value >= 0.0, 1.0, small) / total
        weight = (jnp.where(match, -scale, scale) * sigmoid).astype(BF16)
        grad = jnp.dot(weight, visited[...], preferred_element_type=F32)
        loss = jnp.sum(losses, axis=1, keepdims=True)
        if not first:
            rows = pl.ds(half * sides[0], half * len(sides))
            grad = grad + grad_in[rows, :]
            loss = loss + loss_in[rows, :]
        if not last:
            outs[0][...] = grad
            outs[1][...] = loss
            return
        loss_row = jnp.transpose(jnp.broadcast_to(loss, (half, LANES)))[0:1]
        if sides[0] == 0:
            grad_keep, grad_own, loss_own = outs
            grad_keep[...] = grad
            grad_own[...] = grad.astype(BF16)
            loss_own[...] = loss_row
        else:
            split_rows(loss_row, extra)
            write_block(outs[0], grad, extra[...])

    return kernel


def finish(grad, unit, norm):
    value = unit[...]
    along = jnp.sum(value * grad, axis=1, keepdims=True)
    return ((grad - value * along) / norm[...]).astype(BF16)


def own_demb_kernel(kept, near, unit, norm, loss_own, out, loss_mine, joined, extra):
    half, width = unit.shape
    read_block(near, joined, 0, half)
    out[pl.ds(0, half), :] = finish(kept[...] + joined[...].astype(F32), unit, norm)
    parts = extra_rows(near)
    loss = loss_own[...] + (parts[0:1] + parts[1:2] + parts[2:3])[:, :half]
    loss_mine[...] = loss
    split_rows(loss, extra)
    out[pl.ds(half, EXTRA), :] = jnp.zeros((EXTRA, width), BF16)
    out[pl.ds(half, EXTRA), pl.ds(0, LANES)] = extra[...].astype(BF16)


def other_demb_kernel(across, diagonal, unit, norm, out, joined):
    read_block(diagonal, joined, 0, unit.shape[0])
    out[...] = finish(across[...].astype(F32) + joined[...].astype(F32), unit, norm)


def grads_kernel(
    own, own_got, other, other_got, loss_mine, image_proj, text_proj,
    pair_loss, image_grad, text_grad, joined,
):
    half = joined.shape[1] // 2
    core = lax.axis_index("mp")

    def tower(index, mine, theirs, proj, grad):
        mine, theirs = mine[pl.ds(0, half), :], theirs[pl.ds(0, half), :]
        joined[index, pl.ds(0, half), :] = jnp.where(core == 0, mine, theirs)
        joined[index, pl.ds(half, half), :] = jnp.where(core == 0, theirs, mine)
        grad[...] = lax.dot_general(
            joined[index], proj[...], NT, preferred_element_type=F32
        ).astype(BF16)

    @pl.when(lax.axis_index("sec") == 0)
    def _():
        tower(0, own, own_got, image_proj, image_grad)
        tower(1, other, other_got, text_proj, text_grad)

    @pl.when(lax.axis_index("sec") != 0)
    def _():
        tower(1, own, own_got, text_proj, text_grad)
        tower(0, other, other_got, image_proj, image_grad)

    parts = own_got[pl.ds(half, EXTRA), pl.ds(0, LANES)].astype(F32)
    loss = loss_mine[...]
    loss_theirs = (parts[0:1] + parts[1:2] + parts[2:3])[:, :half]
    pair_loss[0:1, 0:half] = jnp.where(core == 0, loss, loss_theirs)
    pair_loss[0:1, half : 2 * half] = jnp.where(core == 0, loss_theirs, loss)


def make_per_device(mesh):
    sections = mesh.shape["sec"]
    blocks = mesh.shape["blk"]

    def across_blk(value, step):
        return lax.ppermute(value, "blk", [(i, i ^ step) for i in range(blocks)])

    def per_device(
        image_pooled, text_pooled, image_proj, text_proj, log_multiplier, logit_bias, ids
    ):
        multiplier, bias = log_multiplier[None, :], logit_bias[None, :]
        rows = image_pooled.shape[0]
        half = rows // 2
        width = image_proj.shape[1]
        block_rows = half * (width // LANES) + EXTRA
        whole_f32 = jax.ShapeDtypeStruct((half, width), F32)
        whole_b16 = jax.ShapeDtypeStruct((half, width), BF16)
        block_b16 = jax.ShapeDtypeStruct((block_rows, LANES), BF16)
        norm_shape = jax.ShapeDtypeStruct((half, 1), F32)
        loss_shape = jax.ShapeDtypeStruct((1, half), F32)
        towers = (image_pooled, text_pooled, image_proj, text_proj)
        embed_flops = 2 * half * width * (image_proj.shape[0] + text_proj.shape[0])

        ids_row = ids[None, :]
        copies = max(
            len(cuts(rows)) + len(cuts(proj.shape[0])) for proj in (image_proj, text_proj)
        )
        held = [pltpu.with_memory_space_constraint(t, pltpu.HBM) for t in towers]
        own_sent, *towers = local_call(
            own_sent_kernel,
            "own_sent",
            [whole_b16] + [jax.ShapeDtypeStruct(t.shape, t.dtype) for t in towers],
            [],
            scratch=[pltpu.SemaphoreType.DMA((copies,))],
            flops=embed_flops // 2,
            held=held,
        )
        own_got = lax.ppermute(own_sent, "mp", SWAP)
        (own_kept,) = local_call(
            own_kept_kernel, "own_kept", [whole_f32], towers, flops=embed_flops // 2
        )
        (own_send,) = local_call(join_cores_kernel, "own_send", [whole_b16], [own_kept, own_got])
        other_summed = lax.ppermute(own_send, "sec", SWAP)
        other_sent, other_kept, image_proj, text_proj = local_call(
            other_embed_kernel,
            "other_embed",
            [whole_b16, whole_f32]
            + [jax.ShapeDtypeStruct(t.shape, t.dtype) for t in towers[2:]],
            [*towers, own_send],
            scratch=[pltpu.VMEM(t.shape, t.dtype) for t in towers[:2]]
            + [pltpu.SemaphoreType.DMA((copies,))],
            flops=embed_flops,
            held=held,
            aliases={2: 2, 3: 3},
        )
        other_got = lax.ppermute(other_sent, "mp", SWAP)
        (other_send,) = local_call(
            join_cores_kernel, "other_send", [whole_b16], [other_kept, other_got]
        )
        own_summed = lax.ppermute(other_send, "sec", SWAP)
        (other_summed,) = local_call(
            relay_kernel, "relay", [whole_b16], [other_summed], flops=10**9
        )
        other_unit, visit, other_norm = local_call(
            unit_kernel(False),
            "other_unit",
            [whole_f32, block_b16, norm_shape],
            [other_kept, other_got, other_summed, ids_row],
            scratch=[pltpu.VMEM((EXTRA, LANES), F32)],
        )
        own_unit, own_block, own_norm, params = local_call(
            unit_kernel(True),
            "own_unit",
            [whole_f32, block_b16, norm_shape, jax.ShapeDtypeStruct((2, LANES), F32)],
            [own_kept, own_got, own_summed, ids_row, multiplier, bias],
            scratch=[pltpu.VMEM((EXTRA, LANES), F32)],
        )

        steps = list(range(0, blocks, 2))
        mine = [visit] + [across_blk(visit, k) for k in steps[1:]]
        near_block = across_blk(own_block, 1)
        mine = [visit] + [lax.optimization_barrier((v, own_block))[0] for v in mine[1:]]
        mine[-1:] = local_call(relay_kernel, "relay", [block_b16], [mine[-1]], flops=10**9)
        theirs = [lax.ppermute(v, "mp", SWAP) for v in mine]

        early = list(range(len(steps) - 1))
        groups = [early[i : i + 3] for i in range(0, len(early), 3)] + [[len(steps) - 1]]
        state = []
        for index, group in enumerate(groups):
            first, last = index == 0, index == len(groups) - 1
            pieces = [p for g in group for p in (mine[g], theirs[g])]
            visited_rows = 2 * half * len(group)

            def score(sides, outs):
                sources = [(own_block, near_block)[side] for side in sides]
                return local_call(
                    pair_kernel(len(group), sides, first, last),
                    "pairs",
                    outs,
                    [params, *sources, *pieces, *state],
                    scratch=[
                        pltpu.VMEM((len(sides) * half, width), BF16),
                        pltpu.VMEM((visited_rows, width), BF16),
                        pltpu.VMEM((8, visited_rows), F32),
                        pltpu.VMEM((EXTRA, LANES), F32),
                    ],
                    flops=4 * len(sides) * half * visited_rows * width,
                    transcendentals=3 * len(sides) * half * visited_rows,
                )

            if last:
                grad_keep, grad_own, loss_own = score((0,), [whole_f32, whole_b16, loss_shape])
                (grad_near,) = score((1,), [block_b16])
            else:
                state = score(
                    (0, 1),
                    [
                        jax.ShapeDtypeStruct((2 * half, width), F32),
                        jax.ShapeDtypeStruct((2 * half, 1), F32),
                    ],
                )

        pairs = [(s, b) for s in range(sections) for b in range(blocks)]
        diagonal_pairs = [
            (s * blocks + b, (1 - s) * blocks + (b ^ 1)) for s, b in pairs
        ]
        diagonal = lax.ppermute(grad_near, ("sec", "blk"), diagonal_pairs)
        near = across_blk(grad_near, 1)
        across = lax.ppermute(grad_own, "sec", SWAP)
        own_demb, loss_mine = local_call(
            own_demb_kernel,
            "own_demb",
            [jax.ShapeDtypeStruct((half + EXTRA, width), BF16), loss_shape],
            [grad_keep, near, own_unit, own_norm, loss_own],
            scratch=[pltpu.VMEM((half, width), BF16), pltpu.VMEM((EXTRA, LANES), F32)],
        )
        demb_got = lax.ppermute(own_demb, "mp", SWAP)
        (other_demb,) = local_call(
            other_demb_kernel,
            "other_demb",
            [whole_b16],
            [across, diagonal, other_unit, other_norm],
            scratch=[pltpu.VMEM((half, width), BF16)],
        )
        other_demb_got = lax.ppermute(other_demb, "mp", SWAP)
        return local_call(
            grads_kernel,
            "grads",
            [
                jax.ShapeDtypeStruct((1, rows), F32),
                jax.ShapeDtypeStruct((rows, image_proj.shape[0]), BF16),
                jax.ShapeDtypeStruct((rows, text_proj.shape[0]), BF16),
            ],
            [own_demb, demb_got, other_demb, other_demb_got, loss_mine, image_proj, text_proj],
            scratch=[pltpu.VMEM((2, rows, width), BF16)],
            flops=2 * embed_flops,
        )

    return per_device


def solution(mesh):
    placed = (
        P("blk", ("sec", "mp")),
        P("blk", ("sec", "mp")),
        P(("sec", "mp"), None),
        P(("sec", "mp"), None),
        P(),
        P(),
        P("blk"),
    )
    return jax.shard_map(
        make_per_device(mesh),
        mesh=mesh,
        in_specs=placed,
        out_specs=(P("sec", "blk"), P("blk", ("sec", "mp")), P("blk", ("sec", "mp"))),
        check_vma=False,
    )
```

```python
import jax
import jax.numpy as jnp
from jax import lax
from jax.experimental import pallas as pl
from jax.experimental.pallas import tpu as pltpu
from jax.sharding import PartitionSpec as P

F32 = jnp.float32
BF16 = jnp.bfloat16
SWAP = [(0, 1), (1, 0)]
NT = (((1,), (1,)), ((), ()))
VMEM_LIMIT = 16 * 1024 * 1024
LANES = 128
EXTRA = 8


def local_call(
    kernel, name, outs, arrays, scratch=(), flops=0, transcendentals=0, held=(),
    aliases=(),
):
    nbytes = sum(a.size * a.dtype.itemsize for a in (*arrays, *held))
    return pl.pallas_call(
        kernel,
        out_shape=outs,
        in_specs=[pl.BlockSpec(memory_space=pltpu.VMEM)] * len(arrays)
        + [pl.BlockSpec(memory_space=pltpu.HBM)] * len(held),
        out_specs=[pl.BlockSpec(memory_space=pltpu.VMEM)] * len(outs),
        scratch_shapes=list(scratch),
        compiler_params=pltpu.CompilerParams(vmem_limit_bytes=VMEM_LIMIT),
        cost_estimate=pl.CostEstimate(
            flops=flops, bytes_accessed=nbytes, transcendentals=transcendentals
        ),
        name=name,
        input_output_aliases=dict(aliases),
    )(*arrays, *held)


def cuts(rows):
    size = 128 if rows % 128 == 0 else rows
    return [(start, size) for start in range(0, rows, size)]


def own_first(image, text, own, body):
    is_image = (lax.axis_index("sec") == 0) == own
    pl.when(is_image)(lambda: body(*image))
    pl.when(jnp.logical_not(is_image))(lambda: body(*text))


def bring(sources, targets, sems):
    copies = []
    for source, target in zip(sources, targets):
        for start, size in cuts(source.shape[0]):
            rows = pl.ds(start, size)
            sem = sems.at[len(copies)]
            copies.append(pltpu.make_async_copy(source.at[rows], target.at[rows], sem))
            copies[-1].start()
    return copies


def embed(pooled, proj, out, keep):
    half = out.shape[0]
    core = lax.axis_index("mp")
    rows = pl.ds(pl.multiple_of((core if keep else 1 - core) * half, half), half)
    out[...] = jnp.dot(pooled[rows, :], proj[...], preferred_element_type=F32).astype(out.dtype)


def own_sent_kernel(
    image_pooled, text_pooled, image_proj, text_proj,
    sent, image_rows, text_rows, image_held, text_held, sems,
):
    def body(pooled, proj, rows, held):
        for copy in bring((pooled, proj), (rows, held), sems):
            copy.wait()
        embed(rows, held, sent, False)

    image = (image_pooled, image_proj, image_rows, image_held)
    own_first(image, (text_pooled, text_proj, text_rows, text_held), True, body)


def own_kept_kernel(image_rows, text_rows, image_held, text_held, kept):
    own_first(
        (image_rows, image_held),
        (text_rows, text_held),
        True,
        lambda rows, held: embed(rows, held, kept, True),
    )


def other_embed_kernel(
    image_rows_in, text_rows_in, image_held_in, text_held_in, _,
    image_pooled, text_pooled, image_proj, text_proj,
    sent, kept, image_held, text_held, image_rows, text_rows, sems,
):
    def body(pooled, proj, rows, held):
        for copy in bring((pooled, proj), (rows, held), sems):
            copy.wait()
        embed(rows, held, sent, False)
        embed(rows, held, kept, True)

    image = (image_pooled, image_proj, image_rows, image_held)
    own_first(image, (text_pooled, text_proj, text_rows, text_held), False, body)


def join_cores_kernel(kept, got, send):
    send[...] = (kept[...] + got[...].astype(F32)).astype(BF16)


def write_block(block, value, extra):
    half, width = value.shape
    for c in range(width // LANES):
        block[pl.ds(c * half, half), :] = value[:, c * LANES : (c + 1) * LANES].astype(BF16)
    block[pl.ds(half * (width // LANES), EXTRA), :] = extra.astype(BF16)


def read_block(block, target, start, half):
    for c in range(target.shape[1] // LANES):
        target[pl.ds(start, half), pl.ds(c * LANES, LANES)] = block[pl.ds(c * half, half), :]


def extra_rows(block):
    return block[pl.ds(block.shape[0] - EXTRA, EXTRA), :].astype(F32)


def block_ids(block):
    extra = extra_rows(block)
    return extra[0:1] * 128.0 + extra[1:2]


def split_rows(row, extra):
    high = row.astype(BF16).astype(F32)
    rest = row - high
    middle = rest.astype(BF16).astype(F32)
    extra[...] = jnp.zeros_like(extra)
    for index, part in enumerate((high, middle, rest - middle)):
        extra[index : index + 1, 0 : row.shape[1]] = part


def unit_kernel(own):
    def kernel(kept, got, summed, ids, *refs):
        if own:
            multiplier, bias, unit, block, norm, params, extra = refs
            params[0:1, :] = jnp.broadcast_to(jnp.exp(multiplier[...]), (1, LANES))
            params[1:2, :] = jnp.broadcast_to(bias[...], (1, LANES))
        else:
            unit, block, norm, extra = refs
        half = summed.shape[0]
        core = lax.axis_index("mp")
        half_ids = jnp.where(core == 0, ids[0:1, :half], ids[0:1, half : 2 * half])
        extra[...] = jnp.zeros_like(extra)
        extra[0:1, 0:half] = (half_ids >> 7).astype(F32)
        extra[1:2, 0:half] = (half_ids & 127).astype(F32)
        emb = kept[...] + got[...].astype(F32) + summed[...].astype(F32)
        row_norm = jnp.sqrt(jnp.sum(emb * emb, axis=1, keepdims=True) + 1e-06)
        value = emb / row_norm
        unit[...] = value
        norm[...] = row_norm
        write_block(block, value, extra[...])

    return kernel


def relay_kernel(block, out):
    out[...] = block[...]


def pair_kernel(blocks, sides, first, last):
    def kernel(params, *refs):
        sources, refs = refs[: len(sides)], refs[len(sides) :]
        pieces, refs = refs[: 2 * blocks], refs[2 * blocks :]
        if not first:
            (grad_in, loss_in), refs = refs[:2], refs[2:]
        outs, (own, visited, visit_ids, extra) = refs[:-4], refs[-4:]
        half = own.shape[0] // len(sides)
        columns = []
        for index, source in enumerate(sources):
            read_block(source, own, index * half, half)
            square = jnp.broadcast_to(block_ids(source), (LANES, LANES))
            columns.append(jnp.transpose(square)[:half, 0:1])
        ids = jnp.concatenate(columns, axis=0) if len(sides) > 1 else columns[0]
        for index, piece in enumerate(pieces):
            read_block(piece, visited, index * half, half)
            visit_ids[0:1, pl.ds(index * half, half)] = block_ids(piece)[:, :half]
        scale = params[0:1, 0:1]
        scores = (
            scale * lax.dot_general(own[...], visited[...], NT, preferred_element_type=F32)
            + params[1:2, 0:1]
        )
        match = ids == visit_ids[0:1, :]
        value = jnp.where(match, -scores, scores)
        small = jnp.exp(-jnp.abs(value))
        total = 1.0 + small
        losses = jnp.maximum(value, 0.0) + jnp.log(total)
        sigmoid = jnp.where(value >= 0.0, 1.0, small) / total
        weight = (jnp.where(match, -scale, scale) * sigmoid).astype(BF16)
        grad = jnp.dot(weight, visited[...], preferred_element_type=F32)
        loss = jnp.sum(losses, axis=1, keepdims=True)
        if not first:
            rows = pl.ds(half * sides[0], half * len(sides))
            grad = grad + grad_in[rows, :]
            loss = loss + loss_in[rows, :]
        if not last:
            outs[0][...] = grad
            outs[1][...] = loss
            return
        loss_row = jnp.transpose(jnp.broadcast_to(loss, (half, LANES)))[0:1]
        if sides[0] == 0:
            grad_keep, grad_own, loss_own = outs
            grad_keep[...] = grad
            grad_own[...] = grad.astype(BF16)
            loss_own[...] = loss_row
        else:
            split_rows(loss_row, extra)
            write_block(outs[0], grad, extra[...])

    return kernel


def finish(grad, unit, norm):
    value = unit[...]
    along = jnp.sum(value * grad, axis=1, keepdims=True)
    return ((grad - value * along) / norm[...]).astype(BF16)


def own_demb_kernel(kept, near, unit, norm, loss_own, out, loss_mine, joined, extra):
    half, width = unit.shape
    read_block(near, joined, 0, half)
    out[pl.ds(0, half), :] = finish(kept[...] + joined[...].astype(F32), unit, norm)
    parts = extra_rows(near)
    loss = loss_own[...] + (parts[0:1] + parts[1:2] + parts[2:3])[:, :half]
    loss_mine[...] = loss
    split_rows(loss, extra)
    out[pl.ds(half, EXTRA), :] = jnp.zeros((EXTRA, width), BF16)
    out[pl.ds(half, EXTRA), pl.ds(0, LANES)] = extra[...].astype(BF16)


def other_demb_kernel(across, diagonal, unit, norm, out, joined):
    read_block(diagonal, joined, 0, unit.shape[0])
    out[...] = finish(across[...].astype(F32) + joined[...].astype(F32), unit, norm)


def tower_grad(mine, theirs, proj, joined):
    half = joined.shape[0] // 2
    core = lax.axis_index("mp")
    mine, theirs = mine[pl.ds(0, half), :], theirs[pl.ds(0, half), :]
    joined[pl.ds(0, half), :] = jnp.where(core == 0, mine, theirs)
    joined[pl.ds(half, half), :] = jnp.where(core == 0, theirs, mine)
    return lax.dot_general(
        joined[...], proj[...], NT, preferred_element_type=F32
    ).astype(BF16)


def own_grad_kernel(mine, theirs, loss_mine, image_proj, text_proj, pair_loss, grad, joined):
    def body(proj):
        grad[:, pl.ds(0, proj.shape[0])] = tower_grad(mine, theirs, proj, joined)

    own_first((image_proj,), (text_proj,), True, body)
    half = joined.shape[0] // 2
    core = lax.axis_index("mp")
    parts = theirs[pl.ds(half, EXTRA), pl.ds(0, LANES)].astype(F32)
    loss = loss_mine[...]
    loss_theirs = (parts[0:1] + parts[1:2] + parts[2:3])[:, :half]
    pair_loss[0:1, 0:half] = jnp.where(core == 0, loss, loss_theirs)
    pair_loss[0:1, half : 2 * half] = jnp.where(core == 0, loss_theirs, loss)


def grads_kernel(own_grad, mine, theirs, image_proj, text_proj, image_grad, text_grad, joined):
    def body(proj, grad, proj_own, grad_own):
        grad_own[...] = own_grad[:, pl.ds(0, proj_own.shape[0])]
        grad[...] = tower_grad(mine, theirs, proj, joined)

    image, text = (image_proj, image_grad), (text_proj, text_grad)
    own_first((*image, *text), (*text, *image), False, body)


def make_per_device(mesh):
    sections = mesh.shape["sec"]
    blocks = mesh.shape["blk"]

    def across_blk(value, step):
        return lax.ppermute(value, "blk", [(i, i ^ step) for i in range(blocks)])

    def per_device(
        image_pooled, text_pooled, image_proj, text_proj, log_multiplier, logit_bias, ids
    ):
        multiplier, bias = log_multiplier[None, :], logit_bias[None, :]
        rows = image_pooled.shape[0]
        half = rows // 2
        width = image_proj.shape[1]
        block_rows = half * (width // LANES) + EXTRA
        whole_f32 = jax.ShapeDtypeStruct((half, width), F32)
        whole_b16 = jax.ShapeDtypeStruct((half, width), BF16)
        block_b16 = jax.ShapeDtypeStruct((block_rows, LANES), BF16)
        norm_shape = jax.ShapeDtypeStruct((half, 1), F32)
        loss_shape = jax.ShapeDtypeStruct((1, half), F32)
        towers = (image_pooled, text_pooled, image_proj, text_proj)
        embed_flops = 2 * half * width * (image_proj.shape[0] + text_proj.shape[0])

        ids_row = ids[None, :]
        copies = max(
            len(cuts(rows)) + len(cuts(proj.shape[0])) for proj in (image_proj, text_proj)
        )
        held = [pltpu.with_memory_space_constraint(t, pltpu.HBM) for t in towers]
        own_sent, *towers = local_call(
            own_sent_kernel,
            "own_sent",
            [whole_b16] + [jax.ShapeDtypeStruct(t.shape, t.dtype) for t in towers],
            [],
            scratch=[pltpu.SemaphoreType.DMA((copies,))],
            flops=embed_flops // 2,
            held=held,
        )
        own_got = lax.ppermute(own_sent, "mp", SWAP)
        (own_kept,) = local_call(
            own_kept_kernel, "own_kept", [whole_f32], towers, flops=embed_flops // 2
        )
        (own_send,) = local_call(join_cores_kernel, "own_send", [whole_b16], [own_kept, own_got])
        other_summed = lax.ppermute(own_send, "sec", SWAP)
        other_sent, other_kept, image_proj, text_proj = local_call(
            other_embed_kernel,
            "other_embed",
            [whole_b16, whole_f32]
            + [jax.ShapeDtypeStruct(t.shape, t.dtype) for t in towers[2:]],
            [*towers, own_send],
            scratch=[pltpu.VMEM(t.shape, t.dtype) for t in towers[:2]]
            + [pltpu.SemaphoreType.DMA((copies,))],
            flops=embed_flops,
            held=held,
            aliases={2: 2, 3: 3},
        )
        other_got = lax.ppermute(other_sent, "mp", SWAP)
        (other_send,) = local_call(
            join_cores_kernel, "other_send", [whole_b16], [other_kept, other_got]
        )
        own_summed = lax.ppermute(other_send, "sec", SWAP)
        (other_summed,) = local_call(
            relay_kernel, "relay", [whole_b16], [other_summed], flops=10**9
        )
        other_unit, visit, other_norm = local_call(
            unit_kernel(False),
            "other_unit",
            [whole_f32, block_b16, norm_shape],
            [other_kept, other_got, other_summed, ids_row],
            scratch=[pltpu.VMEM((EXTRA, LANES), F32)],
        )
        own_unit, own_block, own_norm, params = local_call(
            unit_kernel(True),
            "own_unit",
            [whole_f32, block_b16, norm_shape, jax.ShapeDtypeStruct((2, LANES), F32)],
            [own_kept, own_got, own_summed, ids_row, multiplier, bias],
            scratch=[pltpu.VMEM((EXTRA, LANES), F32)],
        )

        steps = list(range(0, blocks, 2))
        mine = [visit] + [across_blk(visit, k) for k in steps[1:]]
        near_block = across_blk(own_block, 1)
        mine = [visit] + [lax.optimization_barrier((v, own_block))[0] for v in mine[1:]]
        mine[-1:] = local_call(relay_kernel, "relay", [block_b16], [mine[-1]], flops=10**9)
        theirs = [lax.ppermute(v, "mp", SWAP) for v in mine]

        early = list(range(len(steps) - 1))
        groups = [early[i : i + 3] for i in range(0, len(early), 3)] + [[len(steps) - 1]]
        state = []
        for index, group in enumerate(groups):
            first, last = index == 0, index == len(groups) - 1
            pieces = [p for g in group for p in (mine[g], theirs[g])]
            visited_rows = 2 * half * len(group)

            def score(sides, outs):
                sources = [(own_block, near_block)[side] for side in sides]
                return local_call(
                    pair_kernel(len(group), sides, first, last),
                    "pairs",
                    outs,
                    [params, *sources, *pieces, *state],
                    scratch=[
                        pltpu.VMEM((len(sides) * half, width), BF16),
                        pltpu.VMEM((visited_rows, width), BF16),
                        pltpu.VMEM((8, visited_rows), F32),
                        pltpu.VMEM((EXTRA, LANES), F32),
                    ],
                    flops=4 * len(sides) * half * visited_rows * width,
                    transcendentals=3 * len(sides) * half * visited_rows,
                )

            if last:
                grad_keep, grad_own, loss_own = score((0,), [whole_f32, whole_b16, loss_shape])
                (grad_near,) = score((1,), [block_b16])
            else:
                state = score(
                    (0, 1),
                    [
                        jax.ShapeDtypeStruct((2 * half, width), F32),
                        jax.ShapeDtypeStruct((2 * half, 1), F32),
                    ],
                )

        pairs = [(s, b) for s in range(sections) for b in range(blocks)]
        diagonal_pairs = [
            (s * blocks + b, (1 - s) * blocks + (b ^ 1)) for s, b in pairs
        ]
        diagonal = lax.ppermute(grad_near, ("sec", "blk"), diagonal_pairs)
        near = across_blk(grad_near, 1)
        across = lax.ppermute(grad_own, "sec", SWAP)
        own_demb, loss_mine = local_call(
            own_demb_kernel,
            "own_demb",
            [jax.ShapeDtypeStruct((half + EXTRA, width), BF16), loss_shape],
            [grad_keep, near, own_unit, own_norm, loss_own],
            scratch=[pltpu.VMEM((half, width), BF16), pltpu.VMEM((EXTRA, LANES), F32)],
        )
        demb_got = lax.ppermute(own_demb, "mp", SWAP)
        (other_demb,) = local_call(
            other_demb_kernel,
            "other_demb",
            [whole_b16],
            [across, diagonal, other_unit, other_norm],
            scratch=[pltpu.VMEM((half, width), BF16)],
        )
        other_demb_got = lax.ppermute(other_demb, "mp", SWAP)
        features = (image_proj.shape[0], text_proj.shape[0])
        pair_loss, own_grad = local_call(
            own_grad_kernel,
            "own_grad",
            [
                jax.ShapeDtypeStruct((1, rows), F32),
                jax.ShapeDtypeStruct((rows, max(features)), BF16),
            ],
            [own_demb, demb_got, loss_mine, image_proj, text_proj],
            scratch=[pltpu.VMEM((rows, width), BF16)],
            flops=embed_flops,
        )
        image_grad, text_grad = local_call(
            grads_kernel,
            "grads",
            [jax.ShapeDtypeStruct((rows, count), BF16) for count in features],
            [own_grad, other_demb, other_demb_got, image_proj, text_proj],
            scratch=[pltpu.VMEM((rows, width), BF16)],
            flops=embed_flops,
        )
        return (pair_loss, image_grad, text_grad)

    return per_device


def solution(mesh):
    placed = (
        P("blk", ("sec", "mp")),
        P("blk", ("sec", "mp")),
        P(("sec", "mp"), None),
        P(("sec", "mp"), None),
        P(),
        P(),
        P("blk"),
    )
    return jax.shard_map(
        make_per_device(mesh),
        mesh=mesh,
        in_specs=placed,
        out_specs=(P("sec", "blk"), P("blk", ("sec", "mp")), P("blk", ("sec", "mp"))),
        check_vma=False,
    )
```

```python
import jax
import jax.numpy as jnp
from jax import lax
from jax.experimental import pallas as pl
from jax.experimental.pallas import tpu as pltpu
from jax.sharding import PartitionSpec as P

F32 = jnp.float32
BF16 = jnp.bfloat16
SWAP = [(0, 1), (1, 0)]
NT = (((1,), (1,)), ((), ()))
VMEM_LIMIT = 16 * 1024 * 1024
LANES = 128
EXTRA = 8


def local_call(
    kernel, name, outs, arrays, scratch=(), flops=0, transcendentals=0, held=(),
    aliases=(),
):
    nbytes = sum(a.size * a.dtype.itemsize for a in (*arrays, *held))
    return pl.pallas_call(
        kernel,
        out_shape=outs,
        in_specs=[pl.BlockSpec(memory_space=pltpu.VMEM)] * len(arrays)
        + [pl.BlockSpec(memory_space=pltpu.HBM)] * len(held),
        out_specs=[pl.BlockSpec(memory_space=pltpu.VMEM)] * len(outs),
        scratch_shapes=list(scratch),
        compiler_params=pltpu.CompilerParams(vmem_limit_bytes=VMEM_LIMIT),
        cost_estimate=pl.CostEstimate(
            flops=flops, bytes_accessed=nbytes, transcendentals=transcendentals
        ),
        name=name,
        input_output_aliases=dict(aliases),
    )(*arrays, *held)


def cuts(rows):
    size = 128 if rows % 128 == 0 else rows
    return [(start, size) for start in range(0, rows, size)]


def own_first(image, text, own, body):
    is_image = (lax.axis_index("sec") == 0) == own
    pl.when(is_image)(lambda: body(*image))
    pl.when(jnp.logical_not(is_image))(lambda: body(*text))


def bring(sources, targets, sems):
    copies = []
    for source, target in zip(sources, targets):
        for start, size in cuts(source.shape[0]):
            rows = pl.ds(start, size)
            sem = sems.at[len(copies)]
            copies.append(pltpu.make_async_copy(source.at[rows], target.at[rows], sem))
            copies[-1].start()
    return copies


def embed(pooled, proj, out, keep):
    half = out.shape[0]
    core = lax.axis_index("mp")
    rows = pl.ds(pl.multiple_of((core if keep else 1 - core) * half, half), half)
    out[...] = jnp.dot(pooled[rows, :], proj[...], preferred_element_type=F32).astype(out.dtype)


def own_sent_kernel(
    image_pooled, text_pooled, image_proj, text_proj,
    sent, image_rows, text_rows, image_held, text_held, sems,
):
    def body(pooled, proj, rows, held):
        for copy in bring((pooled, proj), (rows, held), sems):
            copy.wait()
        embed(rows, held, sent, False)

    image = (image_pooled, image_proj, image_rows, image_held)
    own_first(image, (text_pooled, text_proj, text_rows, text_held), True, body)


def own_kept_kernel(image_rows, text_rows, image_held, text_held, kept):
    own_first(
        (image_rows, image_held),
        (text_rows, text_held),
        True,
        lambda rows, held: embed(rows, held, kept, True),
    )


def other_embed_kernel(
    image_rows_in, text_rows_in, image_held_in, text_held_in, _,
    image_pooled, text_pooled, image_proj, text_proj,
    sent, kept, image_held, text_held, image_rows, text_rows, sems,
):
    def body(pooled, proj, rows, held):
        for copy in bring((pooled, proj), (rows, held), sems):
            copy.wait()
        embed(rows, held, sent, False)
        embed(rows, held, kept, True)

    image = (image_pooled, image_proj, image_rows, image_held)
    own_first(image, (text_pooled, text_proj, text_rows, text_held), False, body)


def join_cores_kernel(kept, got, send):
    send[...] = (kept[...] + got[...].astype(F32)).astype(BF16)


def write_block(block, value, extra):
    half, width = value.shape
    for c in range(width // LANES):
        block[pl.ds(c * half, half), :] = value[:, c * LANES : (c + 1) * LANES].astype(BF16)
    block[pl.ds(half * (width // LANES), EXTRA), :] = extra.astype(BF16)


def read_block(block, target, start, half):
    for c in range(target.shape[1] // LANES):
        target[pl.ds(start, half), pl.ds(c * LANES, LANES)] = block[pl.ds(c * half, half), :]


def extra_rows(block):
    return block[pl.ds(block.shape[0] - EXTRA, EXTRA), :].astype(F32)


def block_ids(block):
    extra = extra_rows(block)
    return extra[0:1] * 128.0 + extra[1:2]


def split_rows(row, extra):
    high = row.astype(BF16).astype(F32)
    rest = row - high
    middle = rest.astype(BF16).astype(F32)
    extra[...] = jnp.zeros_like(extra)
    for index, part in enumerate((high, middle, rest - middle)):
        extra[index : index + 1, 0 : row.shape[1]] = part


def unit_kernel(own):
    def kernel(kept, got, summed, ids, *refs):
        if own:
            multiplier, bias, unit, block, norm, params, extra = refs
            params[0:1, :] = jnp.broadcast_to(jnp.exp(multiplier[...]), (1, LANES))
            params[1:2, :] = jnp.broadcast_to(bias[...], (1, LANES))
        else:
            unit, block, norm, extra = refs
        half = summed.shape[0]
        core = lax.axis_index("mp")
        half_ids = jnp.where(core == 0, ids[0:1, :half], ids[0:1, half : 2 * half])
        extra[...] = jnp.zeros_like(extra)
        extra[0:1, 0:half] = (half_ids >> 7).astype(F32)
        extra[1:2, 0:half] = (half_ids & 127).astype(F32)
        emb = kept[...] + got[...].astype(F32) + summed[...].astype(F32)
        row_norm = jnp.sqrt(jnp.sum(emb * emb, axis=1, keepdims=True) + 1e-06)
        value = emb / row_norm
        unit[...] = value
        norm[...] = row_norm
        write_block(block, value, extra[...])

    return kernel


def relay_kernel(block, out):
    out[...] = block[...]


def pair_kernel(blocks, sides, first, last):
    def kernel(params, *refs):
        sources, refs = refs[: len(sides)], refs[len(sides) :]
        pieces, refs = refs[: 2 * blocks], refs[2 * blocks :]
        if not first:
            (grad_in, loss_in), refs = refs[:2], refs[2:]
        outs, (own, visited, visit_ids, extra) = refs[:-4], refs[-4:]
        half = own.shape[0] // len(sides)
        columns = []
        for index, source in enumerate(sources):
            read_block(source, own, index * half, half)
            square = jnp.broadcast_to(block_ids(source), (LANES, LANES))
            columns.append(jnp.transpose(square)[:half, 0:1])
        ids = jnp.concatenate(columns, axis=0) if len(sides) > 1 else columns[0]
        for index, piece in enumerate(pieces):
            read_block(piece, visited, index * half, half)
            visit_ids[0:1, pl.ds(index * half, half)] = block_ids(piece)[:, :half]
        scale = params[0:1, 0:1]
        scores = (
            scale * lax.dot_general(own[...], visited[...], NT, preferred_element_type=F32)
            + params[1:2, 0:1]
        )
        match = ids == visit_ids[0:1, :]
        value = jnp.where(match, -scores, scores)
        small = jnp.exp(-jnp.abs(value))
        total = 1.0 + small
        losses = jnp.maximum(value, 0.0) + jnp.log(total)
        sigmoid = jnp.where(value >= 0.0, 1.0, small) * pl.reciprocal(total)
        weight = (jnp.where(match, -scale, scale) * sigmoid).astype(BF16)
        grad = jnp.dot(weight, visited[...], preferred_element_type=F32)
        loss = jnp.sum(losses, axis=1, keepdims=True)
        if not first:
            rows = pl.ds(half * sides[0], half * len(sides))
            grad = grad + grad_in[rows, :]
            loss = loss + loss_in[rows, :]
        if not last:
            outs[0][...] = grad
            outs[1][...] = loss
            return
        loss_row = jnp.transpose(jnp.broadcast_to(loss, (half, LANES)))[0:1]
        if sides[0] == 0:
            grad_keep, grad_own, loss_own = outs
            grad_keep[...] = grad
            grad_own[...] = grad.astype(BF16)
            loss_own[...] = loss_row
        else:
            split_rows(loss_row, extra)
            write_block(outs[0], grad, extra[...])

    return kernel


def finish(grad, unit, norm):
    value = unit[...]
    along = jnp.sum(value * grad, axis=1, keepdims=True)
    return ((grad - value * along) / norm[...]).astype(BF16)


def own_demb_kernel(kept, near, unit, norm, loss_own, out, loss_mine, joined, extra):
    half, width = unit.shape
    read_block(near, joined, 0, half)
    out[pl.ds(0, half), :] = finish(kept[...] + joined[...].astype(F32), unit, norm)
    parts = extra_rows(near)
    loss = loss_own[...] + (parts[0:1] + parts[1:2] + parts[2:3])[:, :half]
    loss_mine[...] = loss
    split_rows(loss, extra)
    out[pl.ds(half, EXTRA), :] = jnp.zeros((EXTRA, width), BF16)
    out[pl.ds(half, EXTRA), pl.ds(0, LANES)] = extra[...].astype(BF16)


def other_demb_kernel(across, diagonal, unit, norm, out, joined):
    read_block(diagonal, joined, 0, unit.shape[0])
    out[...] = finish(across[...].astype(F32) + joined[...].astype(F32), unit, norm)


def tower_grad(mine, theirs, proj, joined):
    half = joined.shape[0] // 2
    core = lax.axis_index("mp")
    mine, theirs = mine[pl.ds(0, half), :], theirs[pl.ds(0, half), :]
    joined[pl.ds(0, half), :] = jnp.where(core == 0, mine, theirs)
    joined[pl.ds(half, half), :] = jnp.where(core == 0, theirs, mine)
    return lax.dot_general(
        joined[...], proj[...], NT, preferred_element_type=F32
    ).astype(BF16)


def own_grad_kernel(mine, theirs, loss_mine, image_proj, text_proj, pair_loss, grad, joined):
    def body(proj):
        grad[:, pl.ds(0, proj.shape[0])] = tower_grad(mine, theirs, proj, joined)

    own_first((image_proj,), (text_proj,), True, body)
    half = joined.shape[0] // 2
    core = lax.axis_index("mp")
    parts = theirs[pl.ds(half, EXTRA), pl.ds(0, LANES)].astype(F32)
    loss = loss_mine[...]
    loss_theirs = (parts[0:1] + parts[1:2] + parts[2:3])[:, :half]
    pair_loss[0:1, 0:half] = jnp.where(core == 0, loss, loss_theirs)
    pair_loss[0:1, half : 2 * half] = jnp.where(core == 0, loss_theirs, loss)


def grads_kernel(own_grad, mine, theirs, image_proj, text_proj, image_grad, text_grad, joined):
    def body(proj, grad, proj_own, grad_own):
        grad_own[...] = own_grad[:, pl.ds(0, proj_own.shape[0])]
        grad[...] = tower_grad(mine, theirs, proj, joined)

    image, text = (image_proj, image_grad), (text_proj, text_grad)
    own_first((*image, *text), (*text, *image), False, body)


def make_per_device(mesh):
    sections = mesh.shape["sec"]
    blocks = mesh.shape["blk"]

    def across_blk(value, step):
        return lax.ppermute(value, "blk", [(i, i ^ step) for i in range(blocks)])

    def per_device(
        image_pooled, text_pooled, image_proj, text_proj, log_multiplier, logit_bias, ids
    ):
        multiplier, bias = log_multiplier[None, :], logit_bias[None, :]
        rows = image_pooled.shape[0]
        half = rows // 2
        width = image_proj.shape[1]
        block_rows = half * (width // LANES) + EXTRA
        whole_f32 = jax.ShapeDtypeStruct((half, width), F32)
        whole_b16 = jax.ShapeDtypeStruct((half, width), BF16)
        block_b16 = jax.ShapeDtypeStruct((block_rows, LANES), BF16)
        norm_shape = jax.ShapeDtypeStruct((half, 1), F32)
        loss_shape = jax.ShapeDtypeStruct((1, half), F32)
        towers = (image_pooled, text_pooled, image_proj, text_proj)
        embed_flops = 2 * half * width * (image_proj.shape[0] + text_proj.shape[0])

        ids_row = ids[None, :]
        copies = max(
            len(cuts(rows)) + len(cuts(proj.shape[0])) for proj in (image_proj, text_proj)
        )
        held = [pltpu.with_memory_space_constraint(t, pltpu.HBM) for t in towers]
        own_sent, *towers = local_call(
            own_sent_kernel,
            "own_sent",
            [whole_b16] + [jax.ShapeDtypeStruct(t.shape, t.dtype) for t in towers],
            [],
            scratch=[pltpu.SemaphoreType.DMA((copies,))],
            flops=embed_flops // 2,
            held=held,
        )
        own_got = lax.ppermute(own_sent, "mp", SWAP)
        (own_kept,) = local_call(
            own_kept_kernel, "own_kept", [whole_f32], towers, flops=embed_flops // 2
        )
        (own_send,) = local_call(join_cores_kernel, "own_send", [whole_b16], [own_kept, own_got])
        other_summed = lax.ppermute(own_send, "sec", SWAP)
        other_sent, other_kept, image_proj, text_proj = local_call(
            other_embed_kernel,
            "other_embed",
            [whole_b16, whole_f32]
            + [jax.ShapeDtypeStruct(t.shape, t.dtype) for t in towers[2:]],
            [*towers, own_send],
            scratch=[pltpu.VMEM(t.shape, t.dtype) for t in towers[:2]]
            + [pltpu.SemaphoreType.DMA((copies,))],
            flops=embed_flops,
            held=held,
            aliases={2: 2, 3: 3},
        )
        other_got = lax.ppermute(other_sent, "mp", SWAP)
        (other_send,) = local_call(
            join_cores_kernel, "other_send", [whole_b16], [other_kept, other_got]
        )
        own_summed = lax.ppermute(other_send, "sec", SWAP)
        (other_summed,) = local_call(
            relay_kernel, "relay", [whole_b16], [other_summed], flops=10**9
        )
        other_unit, visit, other_norm = local_call(
            unit_kernel(False),
            "other_unit",
            [whole_f32, block_b16, norm_shape],
            [other_kept, other_got, other_summed, ids_row],
            scratch=[pltpu.VMEM((EXTRA, LANES), F32)],
        )
        own_unit, own_block, own_norm, params = local_call(
            unit_kernel(True),
            "own_unit",
            [whole_f32, block_b16, norm_shape, jax.ShapeDtypeStruct((2, LANES), F32)],
            [own_kept, own_got, own_summed, ids_row, multiplier, bias],
            scratch=[pltpu.VMEM((EXTRA, LANES), F32)],
        )

        steps = list(range(0, blocks, 2))
        mine = [visit] + [across_blk(visit, k) for k in steps[1:]]
        near_block = across_blk(own_block, 1)
        mine = [visit] + [lax.optimization_barrier((v, own_block))[0] for v in mine[1:]]
        mine[-1:] = local_call(relay_kernel, "relay", [block_b16], [mine[-1]], flops=10**9)
        theirs = [lax.ppermute(v, "mp", SWAP) for v in mine]

        early = list(range(len(steps) - 1))
        groups = [early[i : i + 3] for i in range(0, len(early), 3)] + [[len(steps) - 1]]
        state = []
        for index, group in enumerate(groups):
            first, last = index == 0, index == len(groups) - 1
            pieces = [p for g in group for p in (mine[g], theirs[g])]
            visited_rows = 2 * half * len(group)

            def score(sides, outs):
                sources = [(own_block, near_block)[side] for side in sides]
                return local_call(
                    pair_kernel(len(group), sides, first, last),
                    "pairs",
                    outs,
                    [params, *sources, *pieces, *state],
                    scratch=[
                        pltpu.VMEM((len(sides) * half, width), BF16),
                        pltpu.VMEM((visited_rows, width), BF16),
                        pltpu.VMEM((8, visited_rows), F32),
                        pltpu.VMEM((EXTRA, LANES), F32),
                    ],
                    flops=4 * len(sides) * half * visited_rows * width,
                    transcendentals=3 * len(sides) * half * visited_rows,
                )

            if last:
                grad_keep, grad_own, loss_own = score((0,), [whole_f32, whole_b16, loss_shape])
                (grad_near,) = score((1,), [block_b16])
            else:
                state = score(
                    (0, 1),
                    [
                        jax.ShapeDtypeStruct((2 * half, width), F32),
                        jax.ShapeDtypeStruct((2 * half, 1), F32),
                    ],
                )

        pairs = [(s, b) for s in range(sections) for b in range(blocks)]
        diagonal_pairs = [
            (s * blocks + b, (1 - s) * blocks + (b ^ 1)) for s, b in pairs
        ]
        diagonal = lax.ppermute(grad_near, ("sec", "blk"), diagonal_pairs)
        near = across_blk(grad_near, 1)
        across = lax.ppermute(grad_own, "sec", SWAP)
        own_demb, loss_mine = local_call(
            own_demb_kernel,
            "own_demb",
            [jax.ShapeDtypeStruct((half + EXTRA, width), BF16), loss_shape],
            [grad_keep, near, own_unit, own_norm, loss_own],
            scratch=[pltpu.VMEM((half, width), BF16), pltpu.VMEM((EXTRA, LANES), F32)],
        )
        demb_got = lax.ppermute(own_demb, "mp", SWAP)
        (other_demb,) = local_call(
            other_demb_kernel,
            "other_demb",
            [whole_b16],
            [across, diagonal, other_unit, other_norm],
            scratch=[pltpu.VMEM((half, width), BF16)],
        )
        other_demb_got = lax.ppermute(other_demb, "mp", SWAP)
        features = (image_proj.shape[0], text_proj.shape[0])
        pair_loss, own_grad = local_call(
            own_grad_kernel,
            "own_grad",
            [
                jax.ShapeDtypeStruct((1, rows), F32),
                jax.ShapeDtypeStruct((rows, max(features)), BF16),
            ],
            [own_demb, demb_got, loss_mine, image_proj, text_proj],
            scratch=[pltpu.VMEM((rows, width), BF16)],
            flops=embed_flops,
        )
        image_grad, text_grad = local_call(
            grads_kernel,
            "grads",
            [jax.ShapeDtypeStruct((rows, count), BF16) for count in features],
            [own_grad, other_demb, other_demb_got, image_proj, text_proj],
            scratch=[pltpu.VMEM((rows, width), BF16)],
            flops=embed_flops,
        )
        return (pair_loss, image_grad, text_grad)

    return per_device


def solution(mesh):
    placed = (
        P("blk", ("sec", "mp")),
        P("blk", ("sec", "mp")),
        P(("sec", "mp"), None),
        P(("sec", "mp"), None),
        P(),
        P(),
        P("blk"),
    )
    return jax.shard_map(
        make_per_device(mesh),
        mesh=mesh,
        in_specs=placed,
        out_specs=(P("sec", "blk"), P("blk", ("sec", "mp")), P("blk", ("sec", "mp"))),
        check_vma=False,
    )
```
